512 devices in a mesh: row: 16 (over y_hi, x, core), col: 32 (over y_lo, z).
Axes of the slice: x: 4, y: 8 (y_hi: 2, y_lo: 4; y = y_hi * 4 + y_lo), z: 8, core: 2. Of those that a mesh axis runs over, the one named last changes fastest.
Arguments:
- covariance: float32 [8192, 8192], P('row', 'col'), may hold values from -8 to 8, as said below
- couplings: float32 [64, 9, 128, 128], P('row'), may hold values from -0.1875 to 0.1875
- block_columns: int32 [64, 9], replicated, may hold values from 0 to 63, as said below
- onsite: float32 [64], replicated, may hold values from 0.04 to 0.2
Outputs:
- new_covariance: float32 [8192, 8192], P('row', 'col')
The draws below stay inside these ranges and needn't reach their ends.
Inputs may be any that keep to these rules, and one draw needn't show every extreme that they name: `block_columns`: each block row's 9 block columns are distinct and lie within 5 blocks of the row, counted cyclically over the 64 blocks; every row has one block column at distance 5 on each side. The covariance is skew-symmetric.
All inputs are finite; a program needn't handle non-finite values.
Results may differ from the reference program's by a relative error of at most 0.0001.
Values sent between devices are 32-bit elements; how exact they have to be, the bound alone decides.
A program may use at most 64 MiB of HBM per device.

```python
import math
import jax
import jax.numpy as jnp
from jax import lax

N = 8192
BLOCK = 128
NNZ = 9
REACH = 5
ITERS = 1
NB = 64


def draw_covariance(key, part):
    base = jax.random.normal(key, (N, N), jnp.float32)
    return ((base - base.T) * 0.70710677).astype(jnp.float32)


def draw_block_columns(key, part):
    interior = 2 * REACH - 1
    scores = jax.random.randint(key, (NB, interior), 0, 2 ** 20, dtype=jnp.int32) * interior
    scores = scores + jnp.arange(interior, dtype=jnp.int32)[None, :]
    ordering = jnp.argsort(scores, axis=1, stable=True).astype(jnp.int32)
    picked = ordering[:, :NNZ - 2] - (REACH - 1)
    outer_ends = jnp.broadcast_to(jnp.array([-REACH, REACH], dtype=jnp.int32), (NB, 2))
    offsets = jnp.concatenate([outer_ends, picked], axis=1)
    row_numbers = jnp.arange(NB, dtype=jnp.int32)[:, None]
    return ((row_numbers + offsets) % NB).astype(jnp.int32)


def steps_of(key, extent, cuts, low, top_value):
    level = 1.0
    for position, shards_of in cuts:
        draws = jax.random.uniform(jax.random.fold_in(jax.random.fold_in(key, 6), position), (shards_of,), jnp.float32, low / len(cuts), top_value / len(cuts))
        level = level * jnp.repeat(jnp.exp(draws), extent[position] // shards_of).reshape((-1,) + (1,) * (len(extent) - 1 - position))
    return level


def bell_draw(stream_key, shape, scale, reach, cuts=(), held_as=jnp.bfloat16):
    values = jax.random.normal(stream_key, shape, jnp.float32) * scale
    if len(cuts) > 0:
        values = steps_of(stream_key, shape, cuts, -0.22, 0.18) * values
    return jnp.clip(values, min=-reach, max=reach).astype(held_as)


def setup_inputs(seed: int = 0) -> dict:
    streams_of = jax.random.split(jax.random.key(seed), 5)
    return {
        "covariance": draw_covariance(jax.random.fold_in(streams_of[4], 71), 0),
        "couplings": bell_draw(streams_of[1], (NB, NNZ, BLOCK, BLOCK), (NNZ * BLOCK) ** -0.5, 0.1875, ((0, 16),), jnp.float32),
        "block_columns": draw_block_columns(jax.random.fold_in(streams_of[4], 71), 0),
        "onsite": jnp.clip(jnp.exp(jax.random.uniform(streams_of[3], (NB,), jnp.float32, math.log(0.04), math.log(0.2))), 0.04, 0.2),
    }


step_size = 0.25


def tendency(matrix, couplings, block_columns, onsite):
    positions = jnp.arange(NB, dtype=jnp.int32)
    shaped = matrix.reshape(NB, BLOCK, NB, BLOCK)
    diagonal = shaped[positions, :, positions, :] * onsite[:, None, None]
    row_blocks = matrix.reshape(NB, BLOCK, N)
    col_blocks = jnp.transpose(matrix.reshape(N, NB, BLOCK), (1, 0, 2))

    def row_product(block_row):
        picked = row_blocks[block_columns[block_row]]
        terms = jnp.einsum("kab,kbn->an", couplings[block_row], picked, precision=lax.Precision.HIGHEST)
        return terms + jnp.einsum("ab,bn->an", diagonal[block_row], row_blocks[block_row], precision=lax.Precision.HIGHEST)

    def col_product(block_row):
        picked = col_blocks[block_columns[block_row]]
        terms = jnp.einsum("knb,kab->na", picked, couplings[block_row], precision=lax.Precision.HIGHEST)
        return terms + jnp.einsum("nb,ab->na", col_blocks[block_row], diagonal[block_row], precision=lax.Precision.HIGHEST)

    left_part = lax.map(row_product, positions).reshape(N, N)
    right_part = jnp.transpose(lax.map(col_product, positions), (1, 0, 2)).reshape(N, N)
    return left_part + right_part


def reference(covariance, couplings, block_columns, onsite):
    current = covariance
    for iteration in range(ITERS):
        middle = 0.5 * (covariance + current)
        current = covariance + step_size * tendency(middle, couplings, block_columns, onsite)
    return current
```

```python
import functools

import jax
import jax.numpy as jnp
from jax import lax
from jax.experimental import pallas as pl
from jax.experimental.pallas import tpu as pltpu
from jax.sharding import PartitionSpec as P

MESH = pl.DeviceIdType.MESH
BLOCK = 128
REACH = 5
ROWB = 4
COLB = 2
BAND = 2 * REACH + 1
EXT = ROWB + 2 * REACH
STEP = 0.25
ZN = 8
YN = 4


def kernel(
    nrow, nb, nnz,
    cov, coup, cols, onsite, out,
    ext, cbuf, dbuf, ehi, elo, hs, lbuf, tbuf,
    load_sem, hsend, hrecv, dsend1, dsend2, drecv, tsend, trecv,
):
    r = lax.axis_index("row")
    c = lax.axis_index("col")
    zz = lax.rem(c, ZN)
    yy = c // ZN
    tr = ROWB * BLOCK

    def rowdev(d):
        return lax.rem(r + d + nrow, nrow), c

    def zdev(k):
        return r, yy * ZN + lax.rem(zz + k, ZN)

    def ydev(k):
        return r, lax.rem(yy + k, YN) * ZN + zz

    mirror = [(c // 2, 2 * r + h) for h in range(2)]
    side = lax.rem(c, 2)
    on_diag = r == c // 2

    barrier = pltpu.get_barrier_semaphore()
    near = [rowdev(d) for d in (-2, -1, 1, 2)]
    near += [zdev(k) for k in range(1, ZN)] + [ydev(k) for k in range(1, YN)]
    for dev in near:
        pl.semaphore_signal(barrier, inc=1, device_id=dev, device_id_type=MESH)
    for h in range(2):
        @pl.when(jnp.logical_not(jnp.logical_and(on_diag, side == h)))
        def _():
            pl.semaphore_signal(barrier, inc=1, device_id=mirror[h], device_id_type=MESH)

    own = pltpu.make_async_copy(cov, ext.at[pl.ds(REACH * BLOCK, tr)], load_sem.at[0])
    own.start()
    load_c = pltpu.make_async_copy(coup, cbuf.at[:, pl.ds(0, nnz)], load_sem.at[1])
    load_c.start()
    cbuf[:, nnz] = jnp.zeros((ROWB, BLOCK, BLOCK), jnp.float32)

    pl.semaphore_wait(barrier, len(near) + 2 - on_diag.astype(jnp.int32))

    halo = []
    plan = [
        (1, 0, tr, BLOCK),
        (-1, 0, tr, (REACH + ROWB) * BLOCK),
        (2, tr - BLOCK, BLOCK, 0),
        (-2, 0, BLOCK, (EXT - 1) * BLOCK),
    ]
    for n, (d, start, size, dst) in enumerate(plan):
        cp = pltpu.make_async_remote_copy(
            src_ref=cov.at[pl.ds(start, size)],
            dst_ref=ext.at[pl.ds(dst, size)],
            send_sem=hsend.at[n], recv_sem=hrecv.at[n],
            device_id=rowdev(d), device_id_type=MESH,
        )
        cp.start()
        halo.append(cp)

    def z_sends(g):
        return [
            pltpu.make_async_remote_copy(
                src_ref=dbuf.at[pl.ds(2 * g, 2)], dst_ref=dbuf.at[pl.ds(2 * g, 2)],
                send_sem=dsend2.at[k - 1], recv_sem=drecv.at[g],
                device_id=zdev(k), device_id_type=MESH,
            )
            for k in range(1, ZN)
        ]

    def y_sends(g):
        return [
            pltpu.make_async_remote_copy(
                src_ref=dbuf.at[pl.ds(2 * g, 2)], dst_ref=dbuf.at[pl.ds(2 * g, 2)],
                send_sem=dsend1.at[k - 1], recv_sem=drecv.at[g],
                device_id=ydev(k), device_id_type=MESH,
            )
            for k in range(1, YN)
        ]

    own_y = yy == r // 4
    for g in range(2):
        is_z = zz == lax.rem(2 * r + g, ZN)
        is_root = jnp.logical_and(is_z, own_y)

        @pl.when(is_root)
        def _():
            copies = []
            for b in range(2):
                cp = pltpu.make_async_copy(
                    cov.at[pl.ds((2 * g + b) * BLOCK, BLOCK), pl.ds(b * BLOCK, BLOCK)],
                    dbuf.at[2 * g + b], load_sem.at[2 + b],
                )
                cp.start()
                copies.append(cp)
            for cp in copies:
                cp.wait()
            for cp in y_sends(g) + z_sends(g):
                cp.start()

    load_c.wait()
    own.wait()

    def split(v):
        hi = v.astype(jnp.bfloat16)
        return hi, (v - hi.astype(jnp.float32)).astype(jnp.bfloat16)

    def put_h(i, t, v):
        hi, lo = split(v)
        hs[pl.ds(i * BLOCK, BLOCK), pl.ds(t * BLOCK, BLOCK)] = hi
        hs[pl.ds(tr + i * BLOCK, BLOCK), pl.ds(t * BLOCK, BLOCK)] = lo

    centre = []
    for i in range(ROWB):
        row = ROWB * r + i
        slots = [
            jnp.bitwise_and(cols[row, k] - row + nb // 2, nb - 1) - nb // 2 + REACH
            for k in range(nnz)
        ]
        for o in range(BAND):
            which = jnp.int32(nnz)
            for k in range(nnz):
                which = jnp.where(slots[k] == o, k, which)
            if o == REACH:
                centre.append(which)
            else:
                put_h(i, i + o, cbuf[i, which])
        for t in range(EXT):
            if t < i or t > i + BAND - 1:
                zero = jnp.zeros((BLOCK, BLOCK), jnp.bfloat16)
                hs[pl.ds(i * BLOCK, BLOCK), pl.ds(t * BLOCK, BLOCK)] = zero
                hs[pl.ds(tr + i * BLOCK, BLOCK), pl.ds(t * BLOCK, BLOCK)] = zero

    def put_e(start, size):
        hi, lo = split(ext[pl.ds(start, size)])
        ehi[pl.ds(start, size)] = hi
        elo[pl.ds(start, size)] = lo

    put_e(REACH * BLOCK, tr)

    for g in range(2):
        is_z = zz == lax.rem(2 * r + g, ZN)
        is_root = jnp.logical_and(is_z, own_y)

        @pl.when(jnp.logical_not(is_root))
        def _():
            z_sends(g)[0].wait_recv()

        @pl.when(jnp.logical_and(is_z, jnp.logical_not(own_y)))
        def _():
            for cp in z_sends(g):
                cp.start()

    for i in range(ROWB):
        put_h(i, i + REACH, cbuf[i, centre[i]] + onsite[ROWB * r + i] * dbuf[i])

    for cp in halo:
        cp.wait_recv()
    put_e(0, REACH * BLOCK)
    put_e((REACH + ROWB) * BLOCK, REACH * BLOCK)

    both = jnp.dot(hs[...], ehi[...], preferred_element_type=jnp.float32)
    low = jnp.dot(hs[pl.ds(0, tr)], elo[...], preferred_element_type=jnp.float32)
    lbuf[...] = both[:tr] + both[tr:] + low

    def swap(i):
        h, b = i // 2, i % 2
        return pltpu.make_async_remote_copy(
            src_ref=lbuf.at[pl.ds(i * BLOCK, BLOCK)], dst_ref=tbuf.at[side, b],
            send_sem=tsend.at[i], recv_sem=trecv.at[side, b],
            device_id=mirror[h], device_id_type=MESH,
        )

    def keep(i):
        return pltpu.make_async_copy(
            lbuf.at[pl.ds(i * BLOCK, BLOCK)], tbuf.at[side, i % 2], trecv.at[side, i % 2]
        )

    for i in range(ROWB):
        mine = jnp.logical_and(on_diag, side == i // 2)

        @pl.when(mine)
        def _():
            keep(i).start()

        @pl.when(jnp.logical_not(mine))
        def _():
            swap(i).start()

    for g in range(2):
        for b in range(2):
            mine = jnp.logical_and(on_diag, side == g)

            @pl.when(mine)
            def _():
                pltpu.make_async_copy(
                    lbuf.at[pl.ds((2 * g + b) * BLOCK, BLOCK)], tbuf.at[g, b], trecv.at[g, b]
                ).wait()

            @pl.when(jnp.logical_not(mine))
            def _():
                pltpu.make_async_remote_copy(
                    src_ref=lbuf.at[pl.ds(0, BLOCK)], dst_ref=tbuf.at[g, b],
                    send_sem=tsend.at[0], recv_sem=trecv.at[g, b],
                    device_id=mirror[g], device_id_type=MESH,
                ).wait_recv()

            rows = pl.ds(g * 2 * BLOCK, 2 * BLOCK)
            lanes = pl.ds(b * BLOCK, BLOCK)
            here = ext[pl.ds((REACH + 2 * g) * BLOCK, 2 * BLOCK), lanes]
            out[rows, lanes] = here + STEP * (lbuf[rows, lanes] - tbuf[g, b].T)

    for cp in halo:
        cp.wait_send()
    for g in range(2):
        is_z = zz == lax.rem(2 * r + g, ZN)

        @pl.when(jnp.logical_and(is_z, own_y))
        def _():
            for cp in y_sends(g):
                cp.wait_send()

        @pl.when(is_z)
        def _():
            for cp in z_sends(g):
                cp.wait_send()
    for i in range(ROWB):
        @pl.when(jnp.logical_not(jnp.logical_and(on_diag, side == i // 2)))
        def _():
            swap(i).wait_send()


def solution(mesh):
    nrow = mesh.shape["row"]

    def on_device(covariance, couplings, block_columns, onsite):
        rows, width = covariance.shape
        nb, nnz = block_columns.shape
        f32, bf16 = jnp.float32, jnp.bfloat16
        dma = pltpu.SemaphoreType.DMA
        return pl.pallas_call(
            functools.partial(kernel, nrow, nb, nnz),
            out_shape=jax.ShapeDtypeStruct((rows, width), f32),
            in_specs=[
                pl.BlockSpec(memory_space=pl.ANY),
                pl.BlockSpec(memory_space=pl.ANY),
                pl.BlockSpec(memory_space=pltpu.SMEM),
                pl.BlockSpec(memory_space=pltpu.SMEM),
            ],
            out_specs=pl.BlockSpec(memory_space=pltpu.VMEM),
            scratch_shapes=[
                pltpu.VMEM((EXT * BLOCK, width), f32),
                pltpu.VMEM((ROWB, nnz + 1, BLOCK, BLOCK), f32),
                pltpu.VMEM((ROWB, BLOCK, BLOCK), f32),
                pltpu.VMEM((EXT * BLOCK, width), bf16),
                pltpu.VMEM((EXT * BLOCK, width), bf16),
                pltpu.VMEM((2 * rows, EXT * BLOCK), bf16),
                pltpu.VMEM((rows, width), f32),
                pltpu.VMEM((2, 2, BLOCK, width), f32),
                dma((4,)), dma((4,)), dma((4,)), dma((YN - 1,)), dma((ZN - 1,)),
                dma((2,)), dma((4,)), dma((2, 2)),
            ],
            compiler_params=pltpu.CompilerParams(
                collective_id=0, has_side_effects=True, vmem_limit_bytes=48 * 2**20
            ),
        )(covariance, couplings, block_columns, onsite)

    return jax.shard_map(
        on_device,
        mesh=mesh,
        in_specs=(P("row", "col"), P("row", None, None, None), P(), P()),
        out_specs=P("row", "col"),
        check_vma=False,
    )
```

```python
import functools

import jax
import jax.numpy as jnp
from jax import lax
from jax.experimental import pallas as pl
from jax.experimental.pallas import tpu as pltpu
from jax.sharding import PartitionSpec as P

MESH = pl.DeviceIdType.MESH
BLOCK = 128
REACH = 5
ROWB = 4
COLB = 2
BAND = 2 * REACH + 1
EXT = ROWB + 2 * REACH
STEP = 0.25
ZN = 8
i32 = jnp.int32


def both(a, b):
    return jnp.logical_and(a, b)


def kernel(
    nrow, nb, nnz,
    cov, coup, cols_h, onsite_h, out,
    cols, onsite, ext, cbuf, dbuf, dterm, ehi, elo, hs, lbuf, rbuf, tbuf,
    load_sem, hsend, hrecv, dsend, drecv, tsend, fsend, rrecv, trecv,
):
    r = lax.axis_index("row")
    c = lax.axis_index("col")
    zz = lax.rem(c, ZN)
    yy = c // ZN
    tr = ROWB * BLOCK
    half = 2 * BLOCK

    def rowdev(d):
        return lax.rem(r + d + nrow, nrow), c

    def is_me(dev):
        return both(dev[0] == r, dev[1] == c)

    def target(rs, cs, h):
        return cs // 2, 2 * rs + h

    def relay(rs, cs):
        return (
            (cs // 16) * 8 + lax.rem(cs // 4, 4) * 2 + lax.rem(rs, 2),
            (rs // 4) * ZN + lax.rem(cs, ZN),
        )

    direct = is_me(relay(r, c))
    sources = [
        ((c // 8) * 4 + 2 * s + lax.rem(r, 2), (r // 4) * ZN + zz) for s in range(2)
    ]
    is_relay = lax.rem(r // 2, 2) == zz // 4
    relays_for = [both(is_relay, jnp.logical_not(is_me(d))) for d in sources]

    loads = [
        pltpu.make_async_copy(coup, cbuf.at[:, pl.ds(0, nnz)], load_sem.at[0]),
        pltpu.make_async_copy(cols_h, cols, load_sem.at[1]),
        pltpu.make_async_copy(onsite_h, onsite, load_sem.at[2]),
    ] + [
        pltpu.make_async_copy(
            cov.at[:, pl.ds(j * BLOCK, BLOCK)], ext.at[j, pl.ds(REACH * BLOCK, tr)],
            load_sem.at[3 + j],
        )
        for j in range(COLB)
    ]
    for cp in loads:
        cp.start()

    barrier = pltpu.get_barrier_semaphore()

    def tell(dev):
        pl.semaphore_signal(barrier, inc=1, device_id=dev, device_id_type=MESH)

    near = [rowdev(d) for d in (-2, -1, 1, 2)]
    root = c // 2
    same_core = lax.rem(r, 2) == lax.rem(root, 2)
    same_x = lax.rem(r // 2, 4) == lax.rem(root // 2, 4)
    is_root = r == root
    hub = both(same_core, same_x)
    leaf = both(same_core, jnp.logical_not(same_x))
    peer = (lax.rem(r + 8, nrow), c)
    pair = (r + 1 - 2 * lax.rem(r, 2), c)
    xdevs = [((r // 8) * 8 + lax.rem(r + 2 * k, 8), c) for k in (1, 3, 2)]
    for dev in near:
        tell(dev)
    @pl.when(leaf)
    def _():
        tell(((r // 8) * 8 + lax.rem(root, 8), c))

    @pl.when(r == lax.rem(root + 8, nrow))
    def _():
        tell(peer)

    for s in range(2):
        @pl.when(relays_for[s])
        def _():
            tell(sources[s])
    for g in range(2):
        origin = (c // 2, 2 * r + g)
        sender = relay(*origin)

        @pl.when(jnp.logical_not(is_me(sender)))
        def _():
            tell(sender)
    expected = len(near) + jnp.where(direct, 0, 1).astype(i32)
    expected = expected + jnp.where(is_root, 1, 0).astype(i32) + jnp.where(hub, 3, 0).astype(i32)
    for h in range(2):
        go = both(direct, jnp.logical_not(is_me(target(r, c, h))))
        expected = expected + jnp.where(go, 1, 0).astype(i32)
        for s in range(2):
            go = both(relays_for[s], jnp.logical_not(is_me(target(*sources[s], h))))
            expected = expected + jnp.where(go, 1, 0).astype(i32)

    cbuf[:, nnz] = jnp.zeros((ROWB, BLOCK, BLOCK), jnp.float32)
    pl.semaphore_wait(barrier, expected)

    plan = [
        (1, 0, tr, BLOCK),
        (-1, 0, tr, (REACH + ROWB) * BLOCK),
        (2, tr - BLOCK, BLOCK, 0),
        (-2, 0, BLOCK, (EXT - 1) * BLOCK),
    ]
    halo = [
        [
            pltpu.make_async_remote_copy(
                src_ref=cov.at[pl.ds(start, size), pl.ds(j * BLOCK, BLOCK)],
                dst_ref=ext.at[j, pl.ds(dst, size)],
                send_sem=hsend.at[j, n], recv_sem=hrecv.at[j, n],
                device_id=rowdev(d), device_id_type=MESH,
            )
            for n, (d, start, size, dst) in enumerate(plan)
        ]
        for j in range(COLB)
    ]

    def fan(devs, first):
        return [
            pltpu.make_async_remote_copy(
                src_ref=dbuf, dst_ref=dbuf, send_sem=dsend.at[first + k], recv_sem=drecv,
                device_id=dev, device_id_type=MESH,
            )
            for k, dev in enumerate(devs)
        ]

    def forward(cond, devs, first, start):
        @pl.when(cond)
        def _():
            for cp in fan(devs, first):
                if start:
                    cp.start()
                else:
                    cp.wait_send()

    def forwards(start, at_root):
        at = is_root if at_root else jnp.logical_not(is_root)
        if at_root:
            forward(at, [peer], 4, start)
        forward(both(hub, at), xdevs, 1, start)
        forward(both(same_core, at), [pair], 0, start)

    first_diag = 2 * lax.rem(c, 2) * BLOCK

    @pl.when(is_root)
    def _():
        copies = [
            pltpu.make_async_copy(
                cov.at[pl.ds(first_diag + b * BLOCK, BLOCK), pl.ds(b * BLOCK, BLOCK)],
                dbuf.at[b], load_sem.at[5 + b],
            )
            for b in range(2)
        ]
        for cp in copies:
            cp.start()
        for cp in copies:
            cp.wait()

    forwards(True, True)

    for j in range(COLB):
        for cp in halo[j]:
            cp.start()

    for cp in loads:
        cp.wait()

    def split(v):
        hi = v.astype(jnp.bfloat16)
        return hi, (v - hi.astype(jnp.float32)).astype(jnp.bfloat16)

    def put_h(i, t, v):
        hi, lo = split(v)
        hs[pl.ds(i * BLOCK, BLOCK), pl.ds(t * BLOCK, BLOCK)] = hi
        hs[pl.ds(tr + i * BLOCK, BLOCK), pl.ds(t * BLOCK, BLOCK)] = lo

    def put_e(j, start, size):
        hi, lo = split(ext[j, pl.ds(start, size)])
        ehi[j, pl.ds(start, size)] = hi
        elo[j, pl.ds(start, size)] = lo

    for i in range(ROWB):
        row = ROWB * r + i
        slots = [
            jnp.bitwise_and(cols[row, k] - row + nb // 2, nb - 1) - nb // 2 + REACH
            for k in range(nnz)
        ]
        for o in range(BAND):
            which = jnp.int32(nnz)
            for k in range(nnz):
                which = jnp.where(slots[k] == o, k, which)
            put_h(i, i + o, cbuf[i, which])
        for t in range(EXT):
            if t < i or t > i + BAND - 1:
                zero = jnp.zeros((BLOCK, BLOCK), jnp.bfloat16)
                hs[pl.ds(i * BLOCK, BLOCK), pl.ds(t * BLOCK, BLOCK)] = zero
                hs[pl.ds(tr + i * BLOCK, BLOCK), pl.ds(t * BLOCK, BLOCK)] = zero

    for j in range(COLB):
        put_e(j, REACH * BLOCK, tr)

    @pl.when(jnp.logical_not(is_root))
    def _():
        fan([pair], 0)[0].wait_recv()

    forwards(True, False)

    def dot_t(a, b):
        return lax.dot_general(
            a, b, (((1,), (1,)), ((), ())), preferred_element_type=jnp.float32
        )

    mid = pl.ds(REACH * BLOCK, tr)
    for j in range(COLB):
        dhi, dlo = split(onsite[COLB * c + j] * dbuf[j])
        yhi = ehi[j, mid]
        dterm[j] = dot_t(yhi, dhi) + dot_t(yhi, dlo) + dot_t(elo[j, mid], dhi)

    def remote(src, dst, ssem, rsem, dev):
        return pltpu.make_async_remote_copy(
            src_ref=src, dst_ref=dst, send_sem=ssem, recv_sem=rsem,
            device_id=dev, device_id_type=MESH,
        )

    def deliver(src, rs, cs, h, j, ssem):
        side = lax.rem(cs, 2)
        dev = target(rs, cs, h)
        mine = is_me(dev)

        @pl.when(mine)
        def _():
            pltpu.make_async_copy(src, tbuf.at[side, j], trecv.at[side, j]).start()

        @pl.when(jnp.logical_not(mine))
        def _():
            remote(src, tbuf.at[side, j], ssem, trecv.at[side, j], dev).start()

    def drain(src, rs, cs, h, j, ssem):
        side = lax.rem(cs, 2)
        dev = target(rs, cs, h)

        @pl.when(jnp.logical_not(is_me(dev)))
        def _():
            remote(src, tbuf.at[side, j], ssem, trecv.at[side, j], dev).wait_send()

    my_slot = lax.rem(r // 2, 2)

    def chunk(h):
        return pl.ds(h * half, half)

    def to_relay(h, j):
        return remote(
            lbuf.at[j, chunk(h)], rbuf.at[my_slot, j, chunk(h)],
            tsend.at[h, j], rrecv.at[my_slot, h, j], relay(r, c),
        )

    for j in range(COLB):
        for cp in halo[j]:
            cp.wait_recv()
        put_e(j, 0, REACH * BLOCK)
        put_e(j, (REACH + ROWB) * BLOCK, REACH * BLOCK)
        p = jnp.dot(hs[...], ehi[j], preferred_element_type=jnp.float32)
        q = jnp.dot(hs[pl.ds(0, tr)], elo[j], preferred_element_type=jnp.float32)
        lbuf[j] = p[:tr] + p[tr:] + q + dterm[j]

        @pl.when(direct)
        def _():
            for h in range(2):
                deliver(lbuf.at[j, chunk(h)], r, c, h, j, tsend.at[h, j])

        @pl.when(jnp.logical_not(direct))
        def _():
            for h in range(2):
                to_relay(h, j).start()

        for s in range(2):
            @pl.when(relays_for[s])
            def _():
                for h in range(2):
                    src = rbuf.at[s, j, chunk(h)]
                    pltpu.make_async_copy(src, src, rrecv.at[s, h, j]).wait()
                    deliver(src, *sources[s], h, j, fsend.at[s, h, j])

    for j in range(COLB):
        for g in range(2):
            dst = tbuf.at[g, j]
            pltpu.make_async_copy(dst, dst, trecv.at[g, j]).wait()
            rows = pl.ds((2 * g + j) * BLOCK, BLOCK)
            here = pl.ds((REACH + 2 * g + j) * BLOCK, BLOCK)
            turned = tbuf[g, j].T
            for b in range(COLB):
                lanes = pl.ds(b * BLOCK, BLOCK)
                mine = lbuf[b, rows] - turned[:, b * BLOCK:(b + 1) * BLOCK]
                out[rows, lanes] = ext[b, here] + STEP * mine

    for j in range(COLB):
        for cp in halo[j]:
            cp.wait_send()
    forwards(False, True)
    forwards(False, False)
    for j in range(COLB):
        for h in range(2):
            @pl.when(direct)
            def _():
                drain(lbuf.at[j, chunk(h)], r, c, h, j, tsend.at[h, j])

            @pl.when(jnp.logical_not(direct))
            def _():
                to_relay(h, j).wait_send()

            for s in range(2):
                @pl.when(relays_for[s])
                def _():
                    drain(rbuf.at[s, j, chunk(h)], *sources[s], h, j, fsend.at[s, h, j])


def solution(mesh):
    nrow = mesh.shape["row"]

    def on_device(covariance, couplings, block_columns, onsite):
        rows, width = covariance.shape
        nb, nnz = block_columns.shape
        f32, bf16 = jnp.float32, jnp.bfloat16
        dma = pltpu.SemaphoreType.DMA
        return pl.pallas_call(
            functools.partial(kernel, nrow, nb, nnz),
            out_shape=jax.ShapeDtypeStruct((rows, width), f32),
            in_specs=[pl.BlockSpec(memory_space=pl.ANY)] * 4,
            out_specs=pl.BlockSpec(memory_space=pltpu.VMEM),
            scratch_shapes=[
                pltpu.SMEM((nb, nnz), jnp.int32),
                pltpu.SMEM((nb,), f32),
                pltpu.VMEM((COLB, EXT * BLOCK, BLOCK), f32),
                pltpu.VMEM((ROWB, nnz + 1, BLOCK, BLOCK), f32),
                pltpu.VMEM((COLB, BLOCK, BLOCK), f32),
                pltpu.VMEM((COLB, rows, BLOCK), f32),
                pltpu.VMEM((COLB, EXT * BLOCK, BLOCK), bf16),
                pltpu.VMEM((COLB, EXT * BLOCK, BLOCK), bf16),
                pltpu.VMEM((2 * rows, EXT * BLOCK), bf16),
                pltpu.VMEM((COLB, rows, BLOCK), f32),
                pltpu.VMEM((2, COLB, rows, BLOCK), f32),
                pltpu.VMEM((2, COLB, 2 * BLOCK, BLOCK), f32),
                dma((7,)), dma((COLB, 4)), dma((COLB, 4)), dma((5,)), dma(()),
                dma((2, COLB)), dma((2, 2, COLB)), dma((2, 2, COLB)), dma((2, COLB)),
            ],
            compiler_params=pltpu.CompilerParams(
                collective_id=0, has_side_effects=True, vmem_limit_bytes=48 * 2**20
            ),
        )(covariance, couplings, block_columns, onsite)

    return jax.shard_map(
        on_device,
        mesh=mesh,
        in_specs=(P("row", "col"), P("row", None, None, None), P(), P()),
        out_specs=P("row", "col"),
        check_vma=False,
    )
```

```python
import functools

import jax
import jax.numpy as jnp
from jax import lax
from jax.experimental import pallas as pl
from jax.experimental.pallas import tpu as pltpu
from jax.sharding import PartitionSpec as P

MESH = pl.DeviceIdType.MESH
BLOCK = 128
REACH = 5
ROWB = 4
COLB = 2
BAND = 2 * REACH + 1
EXT = ROWB + 2 * REACH
STEP = 0.25
ZN = 8
i32 = jnp.int32


def both(a, b):
    return jnp.logical_and(a, b)


def kernel(
    nrow, nb, nnz,
    cov, coup, cols_h, onsite_h, out,
    cols, onsite, ext, cbuf, dbuf, dterm, ehi, elo, hs, lbuf, rbuf, tbuf,
    load_sem, hsend, hrecv, dsend, drecv, tsend, fsend, rrecv, trecv,
):
    r = lax.axis_index("row")
    c = lax.axis_index("col")
    zz = lax.rem(c, ZN)
    yy = c // ZN
    tr = ROWB * BLOCK
    half = 2 * BLOCK

    def rowdev(d):
        return lax.rem(r + d + nrow, nrow), c

    def is_me(dev):
        return both(dev[0] == r, dev[1] == c)

    def target(rs, cs, h):
        return cs // 2, 2 * rs + h

    def same(a, b):
        return both(a[0] == b[0], a[1] == b[1])

    def part(k, cs):
        return lax.rem(cs + 1 - k, 2)

    def relay(k, rs, cs):
        if k == 0:
            return (
                (cs // 16) * 8 + lax.rem(cs // 4, 4) * 2 + lax.rem(rs, 2),
                (rs // 4) * ZN + lax.rem(cs, ZN),
            )
        return (
            (rs // 8) * 8 + lax.rem(cs // 2, 8),
            (cs // ZN) * ZN + lax.rem(2 * rs + part(k, cs), ZN),
        )

    def goal(k, rs, cs):
        return target(rs, cs, part(k, cs))

    def is_direct(k, rs, cs):
        via = relay(k, rs, cs)
        return jnp.logical_or(same(via, (rs, cs)), same(via, goal(k, rs, cs)))

    direct = [is_direct(k, r, c) for k in range(2)]
    sources = [
        [((c // 8) * 4 + 2 * s + lax.rem(r, 2), (r // 4) * ZN + zz) for s in range(2)],
        [((r // 8) * 8 + 4 * s + zz // 2, yy * ZN + lax.rem(r, 4) * 2 + lax.rem(c, 2)) for s in range(2)],
    ]
    at_relay = [lax.rem(r // 2, 2) == zz // 4, lax.rem(r // 4, 2) == lax.rem(yy, 2)]
    serves = [
        [both(at_relay[k], jnp.logical_not(is_direct(k, *sources[k][s]))) for s in range(2)]
        for k in range(2)
    ]

    loads = [
        pltpu.make_async_copy(coup, cbuf.at[:, pl.ds(0, nnz)], load_sem.at[0]),
        pltpu.make_async_copy(cols_h, cols, load_sem.at[1]),
        pltpu.make_async_copy(onsite_h, onsite, load_sem.at[2]),
    ] + [
        pltpu.make_async_copy(
            cov.at[:, pl.ds(j * BLOCK, BLOCK)], ext.at[j, pl.ds(REACH * BLOCK, tr)],
            load_sem.at[3 + j],
        )
        for j in range(COLB)
    ]
    for cp in loads:
        cp.start()

    barrier = pltpu.get_barrier_semaphore()

    def tell(dev):
        pl.semaphore_signal(barrier, inc=1, device_id=dev, device_id_type=MESH)

    near = [rowdev(d) for d in (-2, -1, 1, 2)]
    root = c // 2
    same_core = lax.rem(r, 2) == lax.rem(root, 2)
    same_x = lax.rem(r // 2, 4) == lax.rem(root // 2, 4)
    is_root = r == root
    hub = both(same_core, same_x)
    leaf = both(same_core, jnp.logical_not(same_x))
    peer = (lax.rem(r + 8, nrow), c)
    pair = (r + 1 - 2 * lax.rem(r, 2), c)
    xdevs = [((r // 8) * 8 + lax.rem(r + 2 * k, 8), c) for k in (1, 3, 2)]
    for dev in near:
        tell(dev)
    @pl.when(leaf)
    def _():
        tell(((r // 8) * 8 + lax.rem(root, 8), c))

    @pl.when(r == lax.rem(root + 8, nrow))
    def _():
        tell(peer)

    for k in range(2):
        for s in range(2):
            @pl.when(serves[k][s])
            def _():
                tell(sources[k][s])
    for g in range(2):
        origin = (c // 2, 2 * r + g)
        for k in range(2):
            mine = lax.rem(c + g + 1 - k, 2) == 0
            straight = is_direct(k, *origin)

            @pl.when(both(both(mine, straight), jnp.logical_not(is_me(origin))))
            def _():
                tell(origin)

            @pl.when(both(mine, jnp.logical_not(straight)))
            def _():
                tell(relay(k, *origin))

    def one(cond):
        return jnp.where(cond, 1, 0).astype(i32)

    expected = len(near) + one(is_root) + 3 * one(hub)
    for k in range(2):
        expected = expected + one(jnp.logical_not(both(direct[k], is_me(goal(k, r, c)))))
        for s in range(2):
            expected = expected + one(serves[k][s])

    cbuf[:, nnz] = jnp.zeros((ROWB, BLOCK, BLOCK), jnp.float32)
    pl.semaphore_wait(barrier, expected)

    plan = [
        (1, 0, tr, BLOCK),
        (-1, 0, tr, (REACH + ROWB) * BLOCK),
        (2, tr - BLOCK, BLOCK, 0),
        (-2, 0, BLOCK, (EXT - 1) * BLOCK),
    ]
    halo = [
        [
            pltpu.make_async_remote_copy(
                src_ref=cov.at[pl.ds(start, size), pl.ds(j * BLOCK, BLOCK)],
                dst_ref=ext.at[j, pl.ds(dst, size)],
                send_sem=hsend.at[j, n], recv_sem=hrecv.at[j, n],
                device_id=rowdev(d), device_id_type=MESH,
            )
            for n, (d, start, size, dst) in enumerate(plan)
        ]
        for j in range(COLB)
    ]

    def fan(devs, first):
        return [
            pltpu.make_async_remote_copy(
                src_ref=dbuf, dst_ref=dbuf, send_sem=dsend.at[first + k], recv_sem=drecv,
                device_id=dev, device_id_type=MESH,
            )
            for k, dev in enumerate(devs)
        ]

    def forward(cond, devs, first, start):
        @pl.when(cond)
        def _():
            for cp in fan(devs, first):
                if start:
                    cp.start()
                else:
                    cp.wait_send()

    def forwards(start, at_root):
        at = is_root if at_root else jnp.logical_not(is_root)
        if at_root:
            forward(at, [peer], 4, start)
        forward(both(hub, at), xdevs, 1, start)
        forward(both(same_core, at), [pair], 0, start)

    first_diag = 2 * lax.rem(c, 2) * BLOCK

    @pl.when(is_root)
    def _():
        copies = [
            pltpu.make_async_copy(
                cov.at[pl.ds(first_diag + b * BLOCK, BLOCK), pl.ds(b * BLOCK, BLOCK)],
                dbuf.at[b], load_sem.at[5 + b],
            )
            for b in range(2)
        ]
        for cp in copies:
            cp.start()
        for cp in copies:
            cp.wait()

    forwards(True, True)

    for j in range(COLB):
        for cp in halo[j]:
            cp.start()

    for cp in loads:
        cp.wait()

    def split(v):
        hi = v.astype(jnp.bfloat16)
        return hi, (v - hi.astype(jnp.float32)).astype(jnp.bfloat16)

    def put_h(i, t, v):
        hi, lo = split(v)
        hs[pl.ds(i * BLOCK, BLOCK), pl.ds(t * BLOCK, BLOCK)] = hi
        hs[pl.ds(tr + i * BLOCK, BLOCK), pl.ds(t * BLOCK, BLOCK)] = lo

    def put_e(j, start, size):
        hi, lo = split(ext[j, pl.ds(start, size)])
        ehi[j, pl.ds(start, size)] = hi
        elo[j, pl.ds(start, size)] = lo

    for i in range(ROWB):
        row = ROWB * r + i
        slots = [
            jnp.bitwise_and(cols[k, row] - row + nb // 2, nb - 1) - nb // 2 + REACH
            for k in range(nnz)
        ]
        for o in range(BAND):
            which = jnp.int32(nnz)
            for k in range(nnz):
                which = jnp.where(slots[k] == o, k, which)
            put_h(i, i + o, cbuf[i, which])
        for t in range(EXT):
            if t < i or t > i + BAND - 1:
                zero = jnp.zeros((BLOCK, BLOCK), jnp.bfloat16)
                hs[pl.ds(i * BLOCK, BLOCK), pl.ds(t * BLOCK, BLOCK)] = zero
                hs[pl.ds(tr + i * BLOCK, BLOCK), pl.ds(t * BLOCK, BLOCK)] = zero

    for j in range(COLB):
        put_e(j, REACH * BLOCK, tr)

    @pl.when(jnp.logical_not(is_root))
    def _():
        fan([pair], 0)[0].wait_recv()

    forwards(True, False)

    def dot_t(a, b):
        return lax.dot_general(
            a, b, (((1,), (1,)), ((), ())), preferred_element_type=jnp.float32
        )

    mid = pl.ds(REACH * BLOCK, tr)
    for j in range(COLB):
        dhi, dlo = split(onsite[COLB * c + j] * dbuf[j])
        yhi = ehi[j, mid]
        dterm[j] = dot_t(yhi, dhi) + dot_t(yhi, dlo) + dot_t(elo[j, mid], dhi)

    def remote(src, dst, ssem, rsem, dev):
        return pltpu.make_async_remote_copy(
            src_ref=src, dst_ref=dst, send_sem=ssem, recv_sem=rsem,
            device_id=dev, device_id_type=MESH,
        )

    side = lax.rem(c, 2)

    def deliver(src, dev, j, ssem):
        return remote(src, tbuf.at[side, j], ssem, trecv.at[side, j], dev)

    def mine_of(k, j):
        return lbuf.at[j, pl.ds(part(k, c) * half, half)]

    def straight(k, j):
        return deliver(mine_of(k, j), goal(k, r, c), j, tsend.at[k, j])

    def inside(k, j):
        return pltpu.make_async_copy(mine_of(k, j), tbuf.at[side, j], trecv.at[side, j])

    def to_relay(k, j):
        slot = lax.rem(r // 2, 2) if k == 0 else lax.rem(r // 4, 2)
        return remote(
            mine_of(k, j), rbuf.at[k, slot, j], tsend.at[k, j], rrecv.at[k, slot, j],
            relay(k, r, c),
        )

    def onward(k, s, j):
        return deliver(rbuf.at[k, s, j], goal(k, *sources[k][s]), j, fsend.at[k, s, j])

    at_home = [is_me(goal(k, r, c)) for k in range(2)]

    for j in range(COLB):
        for cp in halo[j]:
            cp.wait_recv()
        put_e(j, 0, REACH * BLOCK)
        put_e(j, (REACH + ROWB) * BLOCK, REACH * BLOCK)
        p = jnp.dot(hs[...], ehi[j], preferred_element_type=jnp.float32)
        q = jnp.dot(hs[pl.ds(0, tr)], elo[j], preferred_element_type=jnp.float32)
        lbuf[j] = p[:tr] + p[tr:] + q + dterm[j]

        for k in range(2):
            @pl.when(at_home[k])
            def _():
                inside(k, j).start()

            @pl.when(both(direct[k], jnp.logical_not(at_home[k])))
            def _():
                straight(k, j).start()

            @pl.when(jnp.logical_not(direct[k]))
            def _():
                to_relay(k, j).start()

        for k in range(2):
            for s in range(2):
                @pl.when(serves[k][s])
                def _():
                    src = rbuf.at[k, s, j]
                    pltpu.make_async_copy(src, src, rrecv.at[k, s, j]).wait()
                    onward(k, s, j).start()

    for j in range(COLB):
        for g in range(2):
            dst = tbuf.at[g, j]
            pltpu.make_async_copy(dst, dst, trecv.at[g, j]).wait()
            rows = pl.ds((2 * g + j) * BLOCK, BLOCK)
            here = pl.ds((REACH + 2 * g + j) * BLOCK, BLOCK)
            turned = tbuf[g, j].T
            for b in range(COLB):
                lanes = pl.ds(b * BLOCK, BLOCK)
                mine = lbuf[b, rows] - turned[:, b * BLOCK:(b + 1) * BLOCK]
                out[rows, lanes] = ext[b, here] + STEP * mine

    for j in range(COLB):
        for cp in halo[j]:
            cp.wait_send()
    forwards(False, True)
    forwards(False, False)
    for j in range(COLB):
        for k in range(2):
            @pl.when(both(direct[k], jnp.logical_not(at_home[k])))
            def _():
                straight(k, j).wait_send()

            @pl.when(jnp.logical_not(direct[k]))
            def _():
                to_relay(k, j).wait_send()

            for s in range(2):
                @pl.when(serves[k][s])
                def _():
                    onward(k, s, j).wait_send()


def solution(mesh):
    nrow = mesh.shape["row"]

    def on_device(covariance, couplings, block_columns, onsite):
        rows, width = covariance.shape
        nb, nnz = block_columns.shape
        f32, bf16 = jnp.float32, jnp.bfloat16
        dma = pltpu.SemaphoreType.DMA
        return pl.pallas_call(
            functools.partial(kernel, nrow, nb, nnz),
            out_shape=jax.ShapeDtypeStruct((rows, width), f32),
            in_specs=[pl.BlockSpec(memory_space=pl.ANY)] * 4,
            out_specs=pl.BlockSpec(memory_space=pltpu.VMEM),
            scratch_shapes=[
                pltpu.SMEM((nnz, nb), jnp.int32),
                pltpu.SMEM((nb,), f32),
                pltpu.VMEM((COLB, EXT * BLOCK, BLOCK), f32),
                pltpu.VMEM((ROWB, nnz + 1, BLOCK, BLOCK), f32),
                pltpu.VMEM((COLB, BLOCK, BLOCK), f32),
                pltpu.VMEM((COLB, rows, BLOCK), f32),
                pltpu.VMEM((COLB, EXT * BLOCK, BLOCK), bf16),
                pltpu.VMEM((COLB, EXT * BLOCK, BLOCK), bf16),
                pltpu.VMEM((2 * rows, EXT * BLOCK), bf16),
                pltpu.VMEM((COLB, rows, BLOCK), f32),
                pltpu.VMEM((2, 2, COLB, 2 * BLOCK, BLOCK), f32),
                pltpu.VMEM((2, COLB, 2 * BLOCK, BLOCK), f32),
                dma((7,)), dma((COLB, 4)), dma((COLB, 4)), dma((5,)), dma(()),
                dma((2, COLB)), dma((2, 2, COLB)), dma((2, 2, COLB)), dma((2, COLB)),
            ],
            compiler_params=pltpu.CompilerParams(
                collective_id=0, has_side_effects=True, vmem_limit_bytes=63 * 2**20
            ),
        )(covariance, couplings, block_columns.T, onsite)

    return jax.shard_map(
        on_device,
        mesh=mesh,
        in_specs=(P("row", "col"), P("row", None, None, None), P(), P()),
        out_specs=P("row", "col"),
        check_vma=False,
    )
```

```python
import functools

import jax
import jax.numpy as jnp
from jax import lax
from jax.experimental import pallas as pl
from jax.experimental.pallas import tpu as pltpu
from jax.sharding import PartitionSpec as P

MESH = pl.DeviceIdType.MESH
BLOCK = 128
REACH = 5
ROWB = 4
COLB = 2
BAND = 2 * REACH + 1
EXT = ROWB + 2 * REACH
STEP = 0.25
ZN = 8
i32 = jnp.int32


def both(a, b):
    return jnp.logical_and(a, b)


def kernel(
    nrow, nb, nnz,
    cov, coup, cols_h, onsite_h, out,
    cols, onsite, ext, cbuf, dbuf, dterm, ehi, elo, hs, lbuf, rbuf, sbuf, tbuf,
    load_sem, hsend, hrecv, csend, csrecv, ssend, dsend, drecv, tsend, fsend, rrecv, trecv, token,
):
    r = lax.axis_index("row")
    c = lax.axis_index("col")
    zz = lax.rem(c, ZN)
    yy = c // ZN
    tr = ROWB * BLOCK
    half = 2 * BLOCK

    def rowdev(d):
        return lax.rem(r + d + nrow, nrow), c

    def is_me(dev):
        return both(dev[0] == r, dev[1] == c)

    def target(rs, cs, h):
        return cs // 2, 2 * rs + h

    def same(a, b):
        return both(a[0] == b[0], a[1] == b[1])

    def part(k, cs):
        return lax.rem(cs + 1 - k, 2)

    def relay(k, rs, cs):
        if k == 0:
            return (
                (cs // 16) * 8 + lax.rem(cs // 4, 4) * 2 + lax.rem(rs, 2),
                (rs // 4) * ZN + lax.rem(cs, ZN),
            )
        return (
            (rs // 8) * 8 + lax.rem(cs // 2, 8),
            (cs // ZN) * ZN + lax.rem(2 * rs + part(k, cs), ZN),
        )

    def goal(k, rs, cs):
        return target(rs, cs, part(k, cs))

    def is_direct(k, rs, cs):
        via = relay(k, rs, cs)
        return jnp.logical_or(same(via, (rs, cs)), same(via, goal(k, rs, cs)))

    direct = [is_direct(k, r, c) for k in range(2)]
    sources = [
        [((c // 8) * 4 + 2 * s + lax.rem(r, 2), (r // 4) * ZN + zz) for s in range(2)],
        [((r // 8) * 8 + 4 * s + zz // 2, yy * ZN + lax.rem(r, 4) * 2 + lax.rem(c, 2)) for s in range(2)],
    ]
    at_relay = [lax.rem(r // 2, 2) == zz // 4, lax.rem(r // 4, 2) == lax.rem(yy, 2)]
    serves = [
        [both(at_relay[k], jnp.logical_not(is_direct(k, *sources[k][s]))) for s in range(2)]
        for k in range(2)
    ]

    loads = [
        pltpu.make_async_copy(coup, cbuf.at[:, pl.ds(0, nnz)], load_sem.at[0]),
        pltpu.make_async_copy(cols_h, cols, load_sem.at[1]),
        pltpu.make_async_copy(onsite_h, onsite, load_sem.at[2]),
    ] + [
        pltpu.make_async_copy(
            cov.at[:, pl.ds(j * BLOCK, BLOCK)], ext.at[j, pl.ds(REACH * BLOCK, tr)],
            load_sem.at[3 + j],
        )
        for j in range(COLB)
    ]
    root = c // 2
    is_root = r == root
    first_diag = 2 * lax.rem(c, 2) * BLOCK
    diag_loads = [
        pltpu.make_async_copy(
            cov.at[pl.ds(first_diag + b * BLOCK, BLOCK), pl.ds(b * BLOCK, BLOCK)],
            dbuf.at[b], load_sem.at[5 + b],
        )
        for b in range(COLB)
    ]

    @pl.when(is_root)
    def _():
        for cp in diag_loads:
            cp.start()

    for cp in loads[1:] + loads[:1]:
        cp.start()

    barrier = pltpu.get_barrier_semaphore()

    def tell(dev):
        pl.semaphore_signal(barrier, inc=1, device_id=dev, device_id_type=MESH)

    near = [rowdev(d) for d in (-2, -1, 1, 2)]
    same_core = lax.rem(r, 2) == lax.rem(root, 2)
    same_x = lax.rem(r // 2, 4) == lax.rem(root // 2, 4)
    hub = both(same_core, same_x)
    leaf = both(same_core, jnp.logical_not(same_x))
    peer = (lax.rem(r + 8, nrow), c)
    pair = (r + 1 - 2 * lax.rem(r, 2), c)
    xdevs = [((r // 8) * 8 + lax.rem(r + 2 * k, 8), c) for k in (1, 3, 2)]
    for dev in near:
        tell(dev)
    @pl.when(leaf)
    def _():
        tell(((r // 8) * 8 + lax.rem(root, 8), c))

    @pl.when(r == lax.rem(root + 8, nrow))
    def _():
        tell(peer)

    for k in range(2):
        for s in range(2):
            @pl.when(serves[k][s])
            def _():
                tell(sources[k][s])
    for g in range(2):
        origin = (c // 2, 2 * r + g)
        for k in range(2):
            mine = lax.rem(c + g + 1 - k, 2) == 0
            straight = is_direct(k, *origin)

            @pl.when(both(both(mine, straight), jnp.logical_not(is_me(origin))))
            def _():
                tell(origin)

            @pl.when(both(mine, jnp.logical_not(straight)))
            def _():
                tell(relay(k, *origin))

    place = lax.rem(r, 8)
    seam_up = place == 7
    seam_down = place == 0
    via_up = place == 5
    via_down = place == 2

    @pl.when(seam_down)
    def _():
        tell(rowdev(-3))

    @pl.when(seam_up)
    def _():
        tell(rowdev(3))

    low, high = r // 8 == 0, r // 8 == 1
    x_low = lax.rem(r // 4, 2) == 0
    x_high = jnp.logical_not(x_low)
    gives = jnp.logical_or(both(both(low, yy == 3), x_low), both(both(high, yy == 0), x_high))
    takes = jnp.logical_or(both(both(low, yy == 2), x_low), both(both(high, yy == 1), x_high))
    giver = (r, c + ZN - 2 * ZN * (r // 8))
    taker = (r, c - ZN + 2 * ZN * (r // 8))

    @pl.when(takes)
    def _():
        tell(giver)

    def one(cond):
        return jnp.where(cond, 1, 0).astype(i32)

    expected = len(near) + one(is_root) + 3 * one(hub) + one(via_up) + one(via_down) + one(gives)
    for k in range(2):
        expected = expected + one(jnp.logical_not(both(direct[k], is_me(goal(k, r, c)))))
        for s in range(2):
            expected = expected + one(serves[k][s])

    cbuf[:, nnz] = jnp.zeros((ROWB, BLOCK, BLOCK), jnp.float32)
    pl.semaphore_wait(barrier, expected)

    even = lax.rem(r, 2) == 0
    top = (REACH + ROWB) * BLOCK

    def remote(src, dst, ssem, rsem, dev):
        return pltpu.make_async_remote_copy(
            src_ref=src, dst_ref=dst, send_sem=ssem, recv_sem=rsem,
            device_id=dev, device_id_type=MESH,
        )

    def own_rows(j, start, size):
        return cov.at[pl.ds(start, size), pl.ds(j * BLOCK, BLOCK)]

    plan = [
        (1, half, half, BLOCK + half),
        (-1, half, half, top + half),
        (1, 0, half, BLOCK),
        (-1, 0, half, top),
        (2, tr - BLOCK, BLOCK, 0),
        (-2, 0, BLOCK, top + tr),
    ]
    odd = jnp.logical_not(even)
    who = [[None] * 4 + [even, odd] for j in range(COLB - 1)]
    who.append([jnp.logical_not(seam_up), jnp.logical_not(seam_down)] * 2 + [even, odd])

    def halo(j, n):
        d, start, size, dst = plan[n]
        return remote(
            own_rows(j, start, size), ext.at[j, pl.ds(dst, size)],
            hsend.at[j, n], hrecv.at[j, n], rowdev(d),
        )

    last = COLB - 1

    def detour(u, up):
        n = 2 * u + (0 if up else 1)
        return remote(
            own_rows(last, plan[n][1], half), sbuf.at[u],
            hsend.at[last, n], csrecv.at[u], rowdev(-2 if up else 2),
        )

    def detour_on(u, up):
        n = 2 * u + (0 if up else 1)
        return remote(
            sbuf.at[u], ext.at[last, pl.ds(plan[n][3], half)],
            ssend.at[u], hrecv.at[last, n], rowdev(3 if up else -3),
        )

    def share(j, up):
        src, dst, n = (4 * BLOCK, 0, 4) if up else (top, top + tr, 5)
        return remote(
            ext.at[j, pl.ds(src, BLOCK)], ext.at[j, pl.ds(dst, BLOCK)],
            csend.at[j], hrecv.at[j, n], pair,
        )

    def when(cond, act):
        if cond is None:
            act()
        else:
            pl.when(cond)(act)

    def halo_wait(j, n):
        dst = ext.at[j, pl.ds(plan[n][3], plan[n][2])]
        pltpu.make_async_copy(dst, dst, hrecv.at[j, n]).wait()

    def fan(devs, first):
        return [
            pltpu.make_async_remote_copy(
                src_ref=dbuf, dst_ref=dbuf, send_sem=dsend.at[first + k], recv_sem=drecv,
                device_id=dev, device_id_type=MESH,
            )
            for k, dev in enumerate(devs)
        ]

    def forward(cond, devs, first, start):
        @pl.when(cond)
        def _():
            for cp in fan(devs, first):
                if start:
                    cp.start()
                else:
                    cp.wait_send()

    def forwards(start, at_root):
        at = is_root if at_root else jnp.logical_not(is_root)
        if at_root:
            forward(at, [peer], 4, start)
        forward(both(hub, at), xdevs, 1, start)
        forward(both(same_core, at), [pair], 0, start)

    @pl.when(is_root)
    def _():
        for cp in diag_loads:
            cp.wait()
        fan([peer], 4)[0].start()

    for u in range(2):
        when(seam_up, lambda: detour(u, True).start())
        when(seam_down, lambda: detour(u, False).start())
    for n in range(len(plan)):
        when(who[0][n], lambda: halo(0, n).start())

    @pl.when(both(hub, jnp.logical_not(is_root)))
    def _():
        fan([pair], 0)[0].wait_recv()

    @pl.when(hub)
    def _():
        for cp in fan(xdevs, 1) + fan([pair], 0):
            cp.start()

    for n in range(len(plan)):
        when(who[1][n], lambda: halo(1, n).start())

    @pl.when(leaf)
    def _():
        fan([pair], 0)[0].wait_recv()
        fan([pair], 0)[0].start()

    for u in range(2):
        def act(up):
            src = sbuf.at[u]
            pltpu.make_async_copy(src, src, csrecv.at[u]).wait()
            detour_on(u, up).start()

        when(via_up, lambda: act(True))
        when(via_down, lambda: act(False))

    for cp in loads:
        cp.wait()

    def split(v):
        hi = v.astype(jnp.bfloat16)
        return hi, (v - hi.astype(jnp.float32)).astype(jnp.bfloat16)

    def put_h(i, t, v):
        hi, lo = split(v)
        hs[pl.ds(i * BLOCK, BLOCK), pl.ds(t * BLOCK, BLOCK)] = hi
        hs[pl.ds(tr + i * BLOCK, BLOCK), pl.ds(t * BLOCK, BLOCK)] = lo

    def put_e(j, start, size):
        hi, lo = split(ext[j, pl.ds(start, size)])
        ehi[j, pl.ds(start, size)] = hi
        elo[j, pl.ds(start, size)] = lo

    for i in range(ROWB):
        row = ROWB * r + i
        slots = [
            jnp.bitwise_and(cols[k, row] - row + nb // 2, nb - 1) - nb // 2 + REACH
            for k in range(nnz)
        ]
        for o in range(BAND):
            which = jnp.int32(nnz)
            for k in range(nnz):
                which = jnp.where(slots[k] == o, k, which)
            put_h(i, i + o, cbuf[i, which])
        for t in range(EXT):
            if t < i or t > i + BAND - 1:
                zero = jnp.zeros((BLOCK, BLOCK), jnp.bfloat16)
                hs[pl.ds(i * BLOCK, BLOCK), pl.ds(t * BLOCK, BLOCK)] = zero
                hs[pl.ds(tr + i * BLOCK, BLOCK), pl.ds(t * BLOCK, BLOCK)] = zero

    for j in range(COLB):
        put_e(j, REACH * BLOCK, tr)

    @pl.when(jnp.logical_not(same_core))
    def _():
        fan([pair], 0)[0].wait_recv()

    def dot_t(a, b):
        return lax.dot_general(
            a, b, (((1,), (1,)), ((), ())), preferred_element_type=jnp.float32
        )

    mid = pl.ds(REACH * BLOCK, tr)
    for j in range(COLB):
        dhi, dlo = split(onsite[COLB * c + j] * dbuf[j])
        yhi = ehi[j, mid]
        dterm[j] = dot_t(yhi, dhi) + dot_t(yhi, dlo) + dot_t(elo[j, mid], dhi)

    side = lax.rem(c, 2)

    def deliver(src, dev, j, ssem):
        return remote(src, tbuf.at[side, j], ssem, trecv.at[side, j], dev)

    def mine_of(k, j):
        return lbuf.at[j, pl.ds(part(k, c) * half, half)]

    def straight(k, j):
        return deliver(mine_of(k, j), goal(k, r, c), j, tsend.at[k, j])

    def inside(k, j):
        return pltpu.make_async_copy(mine_of(k, j), tbuf.at[side, j], trecv.at[side, j])

    def to_relay(k, j):
        slot = lax.rem(r // 2, 2) if k == 0 else lax.rem(r // 4, 2)
        return remote(
            mine_of(k, j), rbuf.at[k, slot, j], tsend.at[k, j], rrecv.at[k, slot, j],
            relay(k, r, c),
        )

    def onward(k, s, j):
        return deliver(rbuf.at[k, s, j], goal(k, *sources[k][s]), j, fsend.at[k, s, j])

    at_home = [is_me(goal(k, r, c)) for k in range(2)]

    for j in range(COLB):
        @pl.when(even)
        def _():
            halo_wait(j, 0)
            share(j, True).start()

        @pl.when(jnp.logical_not(even))
        def _():
            halo_wait(j, 3)
            share(j, False).start()

        for n in range(len(plan)):
            if n == 0:
                when(jnp.logical_not(even), lambda: halo_wait(j, n))
            elif n == 3:
                when(even, lambda: halo_wait(j, n))
            else:
                halo_wait(j, n)
        put_e(j, 0, REACH * BLOCK)
        put_e(j, (REACH + ROWB) * BLOCK, REACH * BLOCK)
        p = jnp.dot(hs[...], ehi[j], preferred_element_type=jnp.float32)
        q = jnp.dot(hs[pl.ds(0, tr)], elo[j], preferred_element_type=jnp.float32)
        lbuf[j] = p[:tr] + p[tr:] + q + dterm[j]

        for k in range(2):
            @pl.when(at_home[k])
            def _():
                inside(k, j).start()

            @pl.when(both(direct[k], jnp.logical_not(at_home[k])))
            def _():
                straight(k, j).start()

            @pl.when(jnp.logical_not(direct[k]))
            def _():
                to_relay(k, j).start()

    def forward_on(k, j):
        for s in range(2):
            @pl.when(serves[k][s])
            def _():
                src = rbuf.at[k, s, j]
                pltpu.make_async_copy(src, src, rrecv.at[k, s, j]).wait()
                onward(k, s, j).start()

    forward_on(0, 0)

    @pl.when(gives)
    def _():
        for j in range(COLB):
            to_relay(0, j).wait_send()
        pl.semaphore_signal(token, inc=1, device_id=taker, device_id_type=MESH)

    forward_on(0, 1)

    @pl.when(takes)
    def _():
        pl.semaphore_wait(token, 1)

    forward_on(1, 0)
    forward_on(1, 1)

    for j in range(COLB):
        for g in range(2):
            dst = tbuf.at[g, j]
            pltpu.make_async_copy(dst, dst, trecv.at[g, j]).wait()
            rows = pl.ds((2 * g + j) * BLOCK, BLOCK)
            here = pl.ds((REACH + 2 * g + j) * BLOCK, BLOCK)
            turned = tbuf[g, j].T
            for b in range(COLB):
                lanes = pl.ds(b * BLOCK, BLOCK)
                mine = lbuf[b, rows] - turned[:, b * BLOCK:(b + 1) * BLOCK]
                out[rows, lanes] = ext[b, here] + STEP * mine

    for j in range(COLB):
        for n in range(len(plan)):
            when(who[j][n], lambda: halo(j, n).wait_send())
        when(even, lambda: share(j, True).wait_send())
        when(jnp.logical_not(even), lambda: share(j, False).wait_send())
    for u in range(2):
        when(seam_up, lambda: detour(u, True).wait_send())
        when(seam_down, lambda: detour(u, False).wait_send())
        when(via_up, lambda: detour_on(u, True).wait_send())
        when(via_down, lambda: detour_on(u, False).wait_send())
    forwards(False, True)
    forwards(False, False)
    for j in range(COLB):
        for k in range(2):
            @pl.when(both(direct[k], jnp.logical_not(at_home[k])))
            def _():
                straight(k, j).wait_send()

            left = jnp.logical_not(direct[k])
            if k == 0:
                left = both(left, jnp.logical_not(gives))

            @pl.when(left)
            def _():
                to_relay(k, j).wait_send()

            for s in range(2):
                @pl.when(serves[k][s])
                def _():
                    onward(k, s, j).wait_send()


def solution(mesh):
    nrow = mesh.shape["row"]

    def on_device(covariance, couplings, block_columns, onsite):
        rows, width = covariance.shape
        nb, nnz = block_columns.shape
        f32, bf16 = jnp.float32, jnp.bfloat16
        dma = pltpu.SemaphoreType.DMA
        return pl.pallas_call(
            functools.partial(kernel, nrow, nb, nnz),
            out_shape=jax.ShapeDtypeStruct((rows, width), f32),
            in_specs=[pl.BlockSpec(memory_space=pl.ANY)] * 4,
            out_specs=pl.BlockSpec(memory_space=pltpu.VMEM),
            scratch_shapes=[
                pltpu.SMEM((nnz, nb), jnp.int32),
                pltpu.SMEM((nb,), f32),
                pltpu.VMEM((COLB, EXT * BLOCK, BLOCK), f32),
                pltpu.VMEM((ROWB, nnz + 1, BLOCK, BLOCK), f32),
                pltpu.VMEM((COLB, BLOCK, BLOCK), f32),
                pltpu.VMEM((COLB, rows, BLOCK), f32),
                pltpu.VMEM((COLB, EXT * BLOCK, BLOCK), bf16),
                pltpu.VMEM((COLB, EXT * BLOCK, BLOCK), bf16),
                pltpu.VMEM((2 * rows, EXT * BLOCK), bf16),
                pltpu.VMEM((COLB, rows, BLOCK), f32),
                pltpu.VMEM((2, 2, COLB, 2 * BLOCK, BLOCK), f32),
                pltpu.VMEM((COLB, 2 * BLOCK, BLOCK), f32),
                pltpu.VMEM((2, COLB, 2 * BLOCK, BLOCK), f32),
                dma((7,)), dma((COLB, 6)), dma((COLB, 6)), dma((COLB,)), dma((2,)), dma((2,)),
                dma((5,)), dma(()),
                dma((2, COLB)), dma((2, 2, COLB)), dma((2, 2, COLB)), dma((2, COLB)),
                pltpu.SemaphoreType.REGULAR,
            ],
            compiler_params=pltpu.CompilerParams(
                collective_id=0, has_side_effects=True, vmem_limit_bytes=63 * 2**20
            ),
        )(covariance, couplings, block_columns.T, onsite)

    return jax.shard_map(
        on_device,
        mesh=mesh,
        in_specs=(P("row", "col"), P("row", None, None, None), P(), P()),
        out_specs=P("row", "col"),
        check_vma=False,
    )
```

```python
import functools

import jax
import jax.numpy as jnp
from jax import lax
from jax.experimental import pallas as pl
from jax.experimental.pallas import tpu as pltpu
from jax.sharding import PartitionSpec as P

MESH = pl.DeviceIdType.MESH
BLOCK = 128
REACH = 5
ROWB = 4
COLB = 2
BAND = 2 * REACH + 1
EXT = ROWB + 2 * REACH
STEP = 0.25
ZN = 8
i32 = jnp.int32


def both(a, b):
    return jnp.logical_and(a, b)


def kernel(
    nrow, nb, nnz,
    cov, coup, cols_h, onsite_h, out,
    cols, onsite, ext, cbuf, dbuf, pbuf, dterm, ehi, elo, hs, lbuf, rbuf, sbuf, tbuf,
    load_sem, hsend, hrecv, csend, csrecv, ssend, dsend, drecv, tsend, fsend, rrecv, trecv, token,
):
    r = lax.axis_index("row")
    c = lax.axis_index("col")
    zz = lax.rem(c, ZN)
    yy = c // ZN
    tr = ROWB * BLOCK
    half = 2 * BLOCK

    def rowdev(d):
        return lax.rem(r + d + nrow, nrow), c

    def is_me(dev):
        return both(dev[0] == r, dev[1] == c)

    def target(rs, cs, h):
        return cs // 2, 2 * rs + h

    def same(a, b):
        return both(a[0] == b[0], a[1] == b[1])

    def part(k, cs):
        return lax.rem(cs + 1 - k, 2)

    def relay(k, rs, cs):
        if k == 0:
            return (
                (cs // 16) * 8 + lax.rem(cs // 4, 4) * 2 + lax.rem(rs, 2),
                (rs // 4) * ZN + lax.rem(cs, ZN),
            )
        return (
            (rs // 8) * 8 + lax.rem(cs // 2, 8),
            (cs // ZN) * ZN + lax.rem(2 * rs + part(k, cs), ZN),
        )

    def goal(k, rs, cs):
        return target(rs, cs, part(k, cs))

    def is_direct(k, rs, cs):
        via = relay(k, rs, cs)
        return jnp.logical_or(same(via, (rs, cs)), same(via, goal(k, rs, cs)))

    direct = [is_direct(k, r, c) for k in range(2)]
    sources = [
        [((c // 8) * 4 + 2 * s + lax.rem(r, 2), (r // 4) * ZN + zz) for s in range(2)],
        [((r // 8) * 8 + 4 * s + zz // 2, yy * ZN + lax.rem(r, 4) * 2 + lax.rem(c, 2)) for s in range(2)],
    ]
    at_relay = [lax.rem(r // 2, 2) == zz // 4, lax.rem(r // 4, 2) == lax.rem(yy, 2)]
    serves = [
        [both(at_relay[k], jnp.logical_not(is_direct(k, *sources[k][s]))) for s in range(2)]
        for k in range(2)
    ]

    loads = [
        pltpu.make_async_copy(coup, cbuf.at[:, pl.ds(0, nnz)], load_sem.at[0]),
        pltpu.make_async_copy(cols_h, cols, load_sem.at[1]),
        pltpu.make_async_copy(onsite_h, onsite, load_sem.at[2]),
    ] + [
        pltpu.make_async_copy(
            cov.at[:, pl.ds(j * BLOCK, BLOCK)], ext.at[j, pl.ds(REACH * BLOCK, tr)],
            load_sem.at[3 + j],
        )
        for j in range(COLB)
    ]
    root = c // 2
    is_root = r == root
    first_diag = 2 * lax.rem(c, 2) * BLOCK
    diag_loads = [
        pltpu.make_async_copy(
            cov.at[pl.ds(first_diag + b * BLOCK, BLOCK), pl.ds(b * BLOCK, BLOCK)],
            dbuf.at[b], load_sem.at[5 + b],
        )
        for b in range(COLB)
    ]

    @pl.when(is_root)
    def _():
        for cp in diag_loads:
            cp.start()

    for cp in loads[1:] + loads[:1]:
        cp.start()

    barrier = pltpu.get_barrier_semaphore()

    def tell(dev):
        pl.semaphore_signal(barrier, inc=1, device_id=dev, device_id_type=MESH)

    near = [rowdev(d) for d in (-2, -1, 1, 2)]
    same_core = lax.rem(r, 2) == lax.rem(root, 2)
    same_x = lax.rem(r // 2, 4) == lax.rem(root // 2, 4)
    hub = both(same_core, same_x)
    leaf = both(same_core, jnp.logical_not(same_x))
    peer = (lax.rem(r + 8, nrow), c)
    pair = (r + 1 - 2 * lax.rem(r, 2), c)
    xdevs = [((r // 8) * 8 + lax.rem(r + 2 * k, 8), c) for k in (1, 3, 2)]
    for dev in near:
        tell(dev)
    @pl.when(leaf)
    def _():
        tell(((r // 8) * 8 + lax.rem(root, 8), c))

    @pl.when(r == lax.rem(root + 8, nrow))
    def _():
        tell(peer)

    for k in range(2):
        for s in range(2):
            @pl.when(serves[k][s])
            def _():
                tell(sources[k][s])
    for g in range(2):
        origin = (c // 2, 2 * r + g)
        for k in range(2):
            mine = lax.rem(c + g + 1 - k, 2) == 0
            straight = is_direct(k, *origin)

            @pl.when(both(both(mine, straight), jnp.logical_not(is_me(origin))))
            def _():
                tell(origin)

            @pl.when(both(mine, jnp.logical_not(straight)))
            def _():
                tell(relay(k, *origin))

    place = lax.rem(r, 8)
    seam_up = place == 7
    seam_down = place == 0
    via_up = place == 5
    via_down = place == 2

    @pl.when(seam_down)
    def _():
        tell(rowdev(-3))

    @pl.when(seam_up)
    def _():
        tell(rowdev(3))

    low, high = r // 8 == 0, r // 8 == 1
    x_low = lax.rem(r // 4, 2) == 0
    x_high = jnp.logical_not(x_low)
    gives = jnp.logical_or(both(both(low, yy == 3), x_low), both(both(high, yy == 0), x_high))
    takes = jnp.logical_or(both(both(low, yy == 2), x_low), both(both(high, yy == 1), x_high))
    giver = (r, c + ZN - 2 * ZN * (r // 8))
    taker = (r, c - ZN + 2 * ZN * (r // 8))

    @pl.when(takes)
    def _():
        tell(giver)

    def one(cond):
        return jnp.where(cond, 1, 0).astype(i32)

    expected = len(near) + one(is_root) + 3 * one(hub) + one(via_up) + one(via_down) + one(gives)
    for k in range(2):
        expected = expected + one(jnp.logical_not(both(direct[k], is_me(goal(k, r, c)))))
        for s in range(2):
            expected = expected + one(serves[k][s])

    hb = BLOCK // 2
    row_of = lax.broadcasted_iota(i32, (hb, BLOCK), 0)
    lane_of = lax.broadcasted_iota(i32, (hb, BLOCK), 1)

    def pack(d):
        return jnp.where(lane_of < row_of, pltpu.roll(d[hb:], hb, 1), d[:hb])

    def unpack(p):
        zero = jnp.zeros_like(p)
        lower = pltpu.roll(jnp.where(lane_of < row_of, p, zero), hb, 1)
        x = jnp.concatenate([jnp.where(lane_of > row_of, p, zero), lower], axis=0)
        return x - x.T

    @pl.when(is_root)
    def _():
        for b, cp in enumerate(diag_loads):
            cp.wait()
            pbuf[b] = pack(dbuf[b])

    cbuf[:, nnz] = jnp.zeros((ROWB, BLOCK, BLOCK), jnp.float32)
    pl.semaphore_wait(barrier, expected)

    even = lax.rem(r, 2) == 0
    top = (REACH + ROWB) * BLOCK

    def remote(src, dst, ssem, rsem, dev):
        return pltpu.make_async_remote_copy(
            src_ref=src, dst_ref=dst, send_sem=ssem, recv_sem=rsem,
            device_id=dev, device_id_type=MESH,
        )

    def own_rows(j, start, size):
        return cov.at[pl.ds(start, size), pl.ds(j * BLOCK, BLOCK)]

    plan = [
        (1, half, half, BLOCK + half),
        (-1, half, half, top + half),
        (1, 0, half, BLOCK),
        (-1, 0, half, top),
        (2, tr - BLOCK, BLOCK, 0),
        (-2, 0, BLOCK, top + tr),
    ]
    odd = jnp.logical_not(even)
    who = [[None] * 4 + [even, odd] for j in range(COLB - 1)]
    who.append([jnp.logical_not(seam_up), jnp.logical_not(seam_down)] * 2 + [even, odd])

    def halo(j, n):
        d, start, size, dst = plan[n]
        return remote(
            own_rows(j, start, size), ext.at[j, pl.ds(dst, size)],
            hsend.at[j, n], hrecv.at[j, n], rowdev(d),
        )

    last = COLB - 1

    def detour(u, up):
        n = 2 * u + (0 if up else 1)
        return remote(
            own_rows(last, plan[n][1], half), sbuf.at[u],
            hsend.at[last, n], csrecv.at[u], rowdev(-2 if up else 2),
        )

    def detour_on(u, up):
        n = 2 * u + (0 if up else 1)
        return remote(
            sbuf.at[u], ext.at[last, pl.ds(plan[n][3], half)],
            ssend.at[u], hrecv.at[last, n], rowdev(3 if up else -3),
        )

    def share(j, up):
        src, dst, n = (4 * BLOCK, 0, 4) if up else (top, top + tr, 5)
        return remote(
            ext.at[j, pl.ds(src, BLOCK)], ext.at[j, pl.ds(dst, BLOCK)],
            csend.at[j], hrecv.at[j, n], pair,
        )

    def when(cond, act):
        if cond is None:
            act()
        else:
            pl.when(cond)(act)

    def halo_wait(j, n):
        dst = ext.at[j, pl.ds(plan[n][3], plan[n][2])]
        pltpu.make_async_copy(dst, dst, hrecv.at[j, n]).wait()

    def fan(devs, first):
        return [
            pltpu.make_async_remote_copy(
                src_ref=pbuf, dst_ref=pbuf, send_sem=dsend.at[first + k], recv_sem=drecv,
                device_id=dev, device_id_type=MESH,
            )
            for k, dev in enumerate(devs)
        ]

    def forward(cond, devs, first, start):
        @pl.when(cond)
        def _():
            for cp in fan(devs, first):
                if start:
                    cp.start()
                else:
                    cp.wait_send()

    def forwards(start, at_root):
        at = is_root if at_root else jnp.logical_not(is_root)
        if at_root:
            forward(at, [peer], 4, start)
        forward(both(hub, at), xdevs, 1, start)
        forward(both(same_core, at), [pair], 0, start)

    @pl.when(is_root)
    def _():
        fan([peer], 4)[0].start()

    for u in range(2):
        when(seam_up, lambda: detour(u, True).start())
        when(seam_down, lambda: detour(u, False).start())
    for n in range(len(plan)):
        when(who[0][n], lambda: halo(0, n).start())

    @pl.when(both(hub, jnp.logical_not(is_root)))
    def _():
        fan([pair], 0)[0].wait_recv()

    @pl.when(hub)
    def _():
        for cp in fan(xdevs, 1) + fan([pair], 0):
            cp.start()

    for n in range(len(plan)):
        when(who[1][n], lambda: halo(1, n).start())

    @pl.when(leaf)
    def _():
        fan([pair], 0)[0].wait_recv()
        fan([pair], 0)[0].start()

    for u in range(2):
        def act(up):
            src = sbuf.at[u]
            pltpu.make_async_copy(src, src, csrecv.at[u]).wait()
            detour_on(u, up).start()

        when(via_up, lambda: act(True))
        when(via_down, lambda: act(False))

    for cp in loads:
        cp.wait()

    def split(v):
        hi = v.astype(jnp.bfloat16)
        return hi, (v - hi.astype(jnp.float32)).astype(jnp.bfloat16)

    def put_h(i, t, v):
        hi, lo = split(v)
        hs[pl.ds(i * BLOCK, BLOCK), pl.ds(t * BLOCK, BLOCK)] = hi
        hs[pl.ds(tr + i * BLOCK, BLOCK), pl.ds(t * BLOCK, BLOCK)] = lo

    def put_e(j, start, size):
        hi, lo = split(ext[j, pl.ds(start, size)])
        ehi[j, pl.ds(start, size)] = hi
        elo[j, pl.ds(start, size)] = lo

    for i in range(ROWB):
        row = ROWB * r + i
        slots = [
            jnp.bitwise_and(cols[k, row] - row + nb // 2, nb - 1) - nb // 2 + REACH
            for k in range(nnz)
        ]
        for o in range(BAND):
            which = jnp.int32(nnz)
            for k in range(nnz):
                which = jnp.where(slots[k] == o, k, which)
            put_h(i, i + o, cbuf[i, which])
        for t in range(EXT):
            if t < i or t > i + BAND - 1:
                zero = jnp.zeros((BLOCK, BLOCK), jnp.bfloat16)
                hs[pl.ds(i * BLOCK, BLOCK), pl.ds(t * BLOCK, BLOCK)] = zero
                hs[pl.ds(tr + i * BLOCK, BLOCK), pl.ds(t * BLOCK, BLOCK)] = zero

    for j in range(COLB):
        put_e(j, REACH * BLOCK, tr)

    @pl.when(jnp.logical_not(same_core))
    def _():
        fan([pair], 0)[0].wait_recv()

    def dot_t(a, b):
        return lax.dot_general(
            a, b, (((1,), (1,)), ((), ())), preferred_element_type=jnp.float32
        )

    mid = pl.ds(REACH * BLOCK, tr)
    for j in range(COLB):
        dhi, dlo = split(onsite[COLB * c + j] * unpack(pbuf[j]))
        yhi = ehi[j, mid]
        dterm[j] = dot_t(yhi, dhi) + dot_t(yhi, dlo) + dot_t(elo[j, mid], dhi)

    side = lax.rem(c, 2)

    def deliver(src, dev, j, ssem):
        return remote(src, tbuf.at[side, j], ssem, trecv.at[side, j], dev)

    def mine_of(k, j):
        return lbuf.at[j, pl.ds(part(k, c) * half, half)]

    def straight(k, j):
        return deliver(mine_of(k, j), goal(k, r, c), j, tsend.at[k, j])

    def inside(k, j):
        return pltpu.make_async_copy(mine_of(k, j), tbuf.at[side, j], trecv.at[side, j])

    def to_relay(k, j):
        slot = lax.rem(r // 2, 2) if k == 0 else lax.rem(r // 4, 2)
        return remote(
            mine_of(k, j), rbuf.at[k, slot, j], tsend.at[k, j], rrecv.at[k, slot, j],
            relay(k, r, c),
        )

    def onward(k, s, j):
        return deliver(rbuf.at[k, s, j], goal(k, *sources[k][s]), j, fsend.at[k, s, j])

    at_home = [is_me(goal(k, r, c)) for k in range(2)]

    def product(j, start, size):
        at = pl.ds(pl.multiple_of(start, BLOCK), size)
        high = ehi[j, at]
        p = jnp.dot(hs[:, at], high, preferred_element_type=jnp.float32)
        q = jnp.dot(hs[pl.ds(0, tr), at], elo[j, at], preferred_element_type=jnp.float32)
        return p[:tr] + p[tr:] + q

    def by_core(a, b):
        return jnp.where(even, a, b).astype(i32)

    for j in range(COLB):
        @pl.when(even)
        def _():
            halo_wait(j, 1)
            halo_wait(j, 3)
            put_e(j, top, tr)

        @pl.when(odd)
        def _():
            halo_wait(j, 0)
            halo_wait(j, 2)
            put_e(j, BLOCK, tr)

        dterm[j] = dterm[j] + product(j, by_core(REACH * BLOCK, BLOCK), 2 * tr)

    for j in range(COLB):
        @pl.when(even)
        def _():
            halo_wait(j, 0)
            share(j, True).start()
            halo_wait(j, 2)
            halo_wait(j, 4)
            put_e(j, 0, REACH * BLOCK)
            halo_wait(j, 5)
            put_e(j, top + tr, BLOCK)

        @pl.when(odd)
        def _():
            halo_wait(j, 3)
            share(j, False).start()
            halo_wait(j, 1)
            halo_wait(j, 5)
            put_e(j, top, REACH * BLOCK)
            halo_wait(j, 4)
            put_e(j, 0, BLOCK)

        far = product(j, by_core(0, top), REACH * BLOCK)
        lbuf[j] = dterm[j] + far + product(j, by_core(top + tr, 0), BLOCK)

        for k in range(2):
            @pl.when(at_home[k])
            def _():
                inside(k, j).start()

            @pl.when(both(direct[k], jnp.logical_not(at_home[k])))
            def _():
                straight(k, j).start()

            @pl.when(jnp.logical_not(direct[k]))
            def _():
                to_relay(k, j).start()

    def forward_on(k, j):
        for s in range(2):
            @pl.when(serves[k][s])
            def _():
                src = rbuf.at[k, s, j]
                pltpu.make_async_copy(src, src, rrecv.at[k, s, j]).wait()
                onward(k, s, j).start()

    forward_on(0, 0)

    @pl.when(gives)
    def _():
        for j in range(COLB):
            to_relay(0, j).wait_send()
        pl.semaphore_signal(token, inc=1, device_id=taker, device_id_type=MESH)

    @pl.when(takes)
    def _():
        forward_on(0, 1)
        pl.semaphore_wait(token, 1)
        forward_on(1, 0)

    @pl.when(jnp.logical_not(takes))
    def _():
        forward_on(1, 0)
        forward_on(0, 1)

    forward_on(1, 1)

    for j in range(COLB):
        for g in range(2):
            dst = tbuf.at[g, j]
            pltpu.make_async_copy(dst, dst, trecv.at[g, j]).wait()
            rows = pl.ds((2 * g + j) * BLOCK, BLOCK)
            here = pl.ds((REACH + 2 * g + j) * BLOCK, BLOCK)
            turned = tbuf[g, j].T
            for b in range(COLB):
                lanes = pl.ds(b * BLOCK, BLOCK)
                mine = lbuf[b, rows] - turned[:, b * BLOCK:(b + 1) * BLOCK]
                out[rows, lanes] = ext[b, here] + STEP * mine

    for j in range(COLB):
        for n in range(len(plan)):
            when(who[j][n], lambda: halo(j, n).wait_send())
        when(even, lambda: share(j, True).wait_send())
        when(jnp.logical_not(even), lambda: share(j, False).wait_send())
    for u in range(2):
        when(seam_up, lambda: detour(u, True).wait_send())
        when(seam_down, lambda: detour(u, False).wait_send())
        when(via_up, lambda: detour_on(u, True).wait_send())
        when(via_down, lambda: detour_on(u, False).wait_send())
    forwards(False, True)
    forwards(False, False)
    for j in range(COLB):
        for k in range(2):
            @pl.when(both(direct[k], jnp.logical_not(at_home[k])))
            def _():
                straight(k, j).wait_send()

            left = jnp.logical_not(direct[k])
            if k == 0:
                left = both(left, jnp.logical_not(gives))

            @pl.when(left)
            def _():
                to_relay(k, j).wait_send()

            for s in range(2):
                @pl.when(serves[k][s])
                def _():
                    onward(k, s, j).wait_send()


def solution(mesh):
    nrow = mesh.shape["row"]

    def on_device(covariance, couplings, block_columns, onsite):
        rows, width = covariance.shape
        nb, nnz = block_columns.shape
        f32, bf16 = jnp.float32, jnp.bfloat16
        dma = pltpu.SemaphoreType.DMA
        return pl.pallas_call(
            functools.partial(kernel, nrow, nb, nnz),
            out_shape=jax.ShapeDtypeStruct((rows, width), f32),
            in_specs=[pl.BlockSpec(memory_space=pl.ANY)] * 4,
            out_specs=pl.BlockSpec(memory_space=pltpu.VMEM),
            scratch_shapes=[
                pltpu.SMEM((nnz, nb), jnp.int32),
                pltpu.SMEM((nb,), f32),
                pltpu.VMEM((COLB, EXT * BLOCK, BLOCK), f32),
                pltpu.VMEM((ROWB, nnz + 1, BLOCK, BLOCK), f32),
                pltpu.VMEM((COLB, BLOCK, BLOCK), f32),
                pltpu.VMEM((COLB, BLOCK // 2, BLOCK), f32),
                pltpu.VMEM((COLB, rows, BLOCK), f32),
                pltpu.VMEM((COLB, EXT * BLOCK, BLOCK), bf16),
                pltpu.VMEM((COLB, EXT * BLOCK, BLOCK), bf16),
                pltpu.VMEM((2 * rows, EXT * BLOCK), bf16),
                pltpu.VMEM((COLB, rows, BLOCK), f32),
                pltpu.VMEM((2, 2, COLB, 2 * BLOCK, BLOCK), f32),
                pltpu.VMEM((COLB, 2 * BLOCK, BLOCK), f32),
                pltpu.VMEM((2, COLB, 2 * BLOCK, BLOCK), f32),
                dma((7,)), dma((COLB, 6)), dma((COLB, 6)), dma((COLB,)), dma((2,)), dma((2,)),
                dma((5,)), dma(()),
                dma((2, COLB)), dma((2, 2, COLB)), dma((2, 2, COLB)), dma((2, COLB)),
                pltpu.SemaphoreType.REGULAR,
            ],
            compiler_params=pltpu.CompilerParams(
                collective_id=0, has_side_effects=True, vmem_limit_bytes=63 * 2**20
            ),
        )(covariance, couplings, block_columns.T, onsite)

    return jax.shard_map(
        on_device,
        mesh=mesh,
        in_specs=(P("row", "col"), P("row", None, None, None), P(), P()),
        out_specs=P("row", "col"),
        check_vma=False,
    )
```

```python
import functools

import jax
import jax.numpy as jnp
from jax import lax
from jax.experimental import pallas as pl
from jax.experimental.pallas import tpu as pltpu
from jax.sharding import PartitionSpec as P

MESH = pl.DeviceIdType.MESH
BLOCK = 128
REACH = 5
ROWB = 4
COLB = 2
BAND = 2 * REACH + 1
EXT = ROWB + 2 * REACH
STEP = 0.25
ZN = 8
i32 = jnp.int32


def both(a, b):
    return jnp.logical_and(a, b)


def kernel(
    nrow, nb, nnz,
    cov, coup, cols_h, onsite_h, out,
    cols, onsite, ext, cbuf, dbuf, pbuf, dterm, ehi, elo, hs, lbuf, rbuf, sbuf, tbuf,
    load_sem, hsend, hrecv, csend, csrecv, ssend, dsend, drecv, tsend, fsend, rrecv, trecv, token, fbuf, frecv, osend,
):
    r = lax.axis_index("row")
    c = lax.axis_index("col")
    zz = lax.rem(c, ZN)
    yy = c // ZN
    tr = ROWB * BLOCK
    half = 2 * BLOCK

    def rowdev(d):
        return lax.rem(r + d + nrow, nrow), c

    def is_me(dev):
        return both(dev[0] == r, dev[1] == c)

    def target(rs, cs, h):
        return cs // 2, 2 * rs + h

    def same(a, b):
        return both(a[0] == b[0], a[1] == b[1])

    def part(k, cs):
        return lax.rem(cs + 1 - k, 2)

    def relay(k, rs, cs):
        if k == 0:
            return (
                (cs // 16) * 8 + lax.rem(cs // 4, 4) * 2 + lax.rem(rs, 2),
                (rs // 4) * ZN + lax.rem(cs, ZN),
            )
        return (
            (rs // 8) * 8 + lax.rem(cs // 2, 8),
            (cs // ZN) * ZN + lax.rem(2 * rs + part(k, cs), ZN),
        )

    def goal(k, rs, cs):
        return target(rs, cs, part(k, cs))

    def is_direct(k, rs, cs):
        via = relay(k, rs, cs)
        return jnp.logical_or(same(via, (rs, cs)), same(via, goal(k, rs, cs)))

    def served(rr, cc, s):
        row = (rr // 8) * 8 + 4 * s + lax.rem(cc, ZN) // 2
        return row, (cc // ZN) * ZN + lax.rem(rr, 4) * 2 + lax.rem(cc, 2)

    def crosses(rr, cc):
        return both(rr // 8 != cc // 16, lax.rem(rr // 4, 2) == rr // 8)

    def around(rr, cc):
        return lax.rem(rr + 8, nrow), 24 - 24 * (rr // 8) + lax.rem(cc, ZN)

    mid = crosses(r, c)
    mid_source = (lax.rem(r + 8, nrow), (lax.rem(r // 4, 2) + 2 * (r // 8)) * ZN + zz)
    far_sources = [served(*mid_source, s) for s in range(2)]
    far_serves = [
        both(both(yy == 3 * (r // 8), crosses(*mid_source)), jnp.logical_not(is_direct(1, *far_sources[s])))
        for s in range(2)
    ]

    direct = [is_direct(k, r, c) for k in range(2)]
    sources = [
        [((c // 8) * 4 + 2 * s + lax.rem(r, 2), (r // 4) * ZN + zz) for s in range(2)],
        [served(r, c, s) for s in range(2)],
    ]
    at_relay = [lax.rem(r // 2, 2) == zz // 4, lax.rem(r // 4, 2) == lax.rem(yy, 2)]
    serves = [
        [both(at_relay[k], jnp.logical_not(is_direct(k, *sources[k][s]))) for s in range(2)]
        for k in range(2)
    ]

    loads = [
        pltpu.make_async_copy(coup, cbuf.at[:, pl.ds(0, nnz)], load_sem.at[0]),
        pltpu.make_async_copy(cols_h, cols, load_sem.at[1]),
        pltpu.make_async_copy(onsite_h, onsite, load_sem.at[2]),
    ] + [
        pltpu.make_async_copy(
            cov.at[:, pl.ds(j * BLOCK, BLOCK)], ext.at[j, pl.ds(REACH * BLOCK, tr)],
            load_sem.at[3 + j],
        )
        for j in range(COLB)
    ]
    root = c // 2
    is_root = r == root
    first_diag = 2 * lax.rem(c, 2) * BLOCK
    diag_loads = [
        pltpu.make_async_copy(
            cov.at[pl.ds(first_diag + b * BLOCK, BLOCK), pl.ds(b * BLOCK, BLOCK)],
            dbuf.at[b], load_sem.at[5 + b],
        )
        for b in range(COLB)
    ]

    @pl.when(is_root)
    def _():
        for cp in diag_loads:
            cp.start()

    for cp in loads[1:] + loads[:1]:
        cp.start()

    barrier = pltpu.get_barrier_semaphore()

    def tell(dev):
        pl.semaphore_signal(barrier, inc=1, device_id=dev, device_id_type=MESH)

    near = [rowdev(d) for d in (-2, -1, 1, 2)]
    same_core = lax.rem(r, 2) == lax.rem(root, 2)
    same_x = lax.rem(r // 2, 4) == lax.rem(root // 2, 4)
    hub = both(same_core, same_x)
    leaf = both(same_core, jnp.logical_not(same_x))
    peer = (lax.rem(r + 8, nrow), c)
    pair = (r + 1 - 2 * lax.rem(r, 2), c)
    xdevs = [((r // 8) * 8 + lax.rem(r + 2 * k, 8), c) for k in (1, 3, 2)]
    for dev in near:
        tell(dev)
    @pl.when(leaf)
    def _():
        tell(((r // 8) * 8 + lax.rem(root, 8), c))

    @pl.when(r == lax.rem(root + 8, nrow))
    def _():
        tell(peer)

    for k in range(2):
        for s in range(2):
            @pl.when(serves[k][s])
            def _():
                tell(sources[k][s])
    for g in range(2):
        origin = (c // 2, 2 * r + g)
        for k in range(2):
            mine = lax.rem(c + g + 1 - k, 2) == 0
            straight = is_direct(k, *origin)

            @pl.when(both(both(mine, straight), jnp.logical_not(is_me(origin))))
            def _():
                tell(origin)

            @pl.when(both(mine, jnp.logical_not(straight)))
            def _():
                tell(relay(k, *origin))

            if k == 1:
                @pl.when(both(both(mine, jnp.logical_not(straight)), crosses(*relay(k, *origin))))
                def _():
                    tell(around(*relay(k, *origin)))

    for s in range(2):
        @pl.when(far_serves[s])
        def _():
            tell(mid_source)

    place = lax.rem(r, 8)
    seam_up = place == 7
    seam_down = place == 0
    via_up = place == 5
    via_down = place == 2

    @pl.when(seam_down)
    def _():
        tell(rowdev(-3))

    @pl.when(seam_up)
    def _():
        tell(rowdev(3))

    low, high = r // 8 == 0, r // 8 == 1
    x_low = lax.rem(r // 4, 2) == 0
    x_high = jnp.logical_not(x_low)
    gives = jnp.logical_or(both(both(low, yy == 3), x_low), both(both(high, yy == 0), x_high))
    takes = jnp.logical_or(both(both(low, yy == 2), x_low), both(both(high, yy == 1), x_high))
    giver = (r, c + ZN - 2 * ZN * (r // 8))
    taker = (r, c - ZN + 2 * ZN * (r // 8))

    @pl.when(takes)
    def _():
        tell(giver)

    def one(cond):
        return jnp.where(cond, 1, 0).astype(i32)

    expected = len(near) + one(is_root) + 3 * one(hub) + one(via_up) + one(via_down) + one(gives)
    for k in range(2):
        expected = expected + one(jnp.logical_not(both(direct[k], is_me(goal(k, r, c)))))
        for s in range(2):
            expected = expected + one(serves[k][s])
    for s in range(2):
        expected = expected + one(both(mid, serves[1][s])) + one(far_serves[s])

    hb = BLOCK // 2
    row_of = lax.broadcasted_iota(i32, (hb, BLOCK), 0)
    lane_of = lax.broadcasted_iota(i32, (hb, BLOCK), 1)

    def pack(d):
        return jnp.where(lane_of < row_of, pltpu.roll(d[hb:], hb, 1), d[:hb])

    def unpack(p):
        zero = jnp.zeros_like(p)
        lower = pltpu.roll(jnp.where(lane_of < row_of, p, zero), hb, 1)
        x = jnp.concatenate([jnp.where(lane_of > row_of, p, zero), lower], axis=0)
        return x - x.T

    @pl.when(is_root)
    def _():
        for b, cp in enumerate(diag_loads):
            cp.wait()
            pbuf[b] = pack(dbuf[b])

    cbuf[:, nnz] = jnp.zeros((ROWB, BLOCK, BLOCK), jnp.float32)
    pl.semaphore_wait(barrier, expected)

    even = lax.rem(r, 2) == 0
    top = (REACH + ROWB) * BLOCK

    def remote(src, dst, ssem, rsem, dev):
        return pltpu.make_async_remote_copy(
            src_ref=src, dst_ref=dst, send_sem=ssem, recv_sem=rsem,
            device_id=dev, device_id_type=MESH,
        )

    def own_rows(j, start, size):
        return cov.at[pl.ds(start, size), pl.ds(j * BLOCK, BLOCK)]

    plan = [
        (1, half, half, BLOCK + half),
        (-1, half, half, top + half),
        (1, 0, half, BLOCK),
        (-1, 0, half, top),
        (2, tr - BLOCK, BLOCK, 0),
        (-2, 0, BLOCK, top + tr),
    ]
    odd = jnp.logical_not(even)
    who = [[None] * 4 + [even, odd] for j in range(COLB - 1)]
    who.append([jnp.logical_not(seam_up), jnp.logical_not(seam_down)] * 2 + [even, odd])

    def halo(j, n):
        d, start, size, dst = plan[n]
        return remote(
            own_rows(j, start, size), ext.at[j, pl.ds(dst, size)],
            hsend.at[j, n], hrecv.at[j, n], rowdev(d),
        )

    last = COLB - 1

    def detour(u, up):
        n = 2 * u + (0 if up else 1)
        return remote(
            own_rows(last, plan[n][1], half), sbuf.at[u],
            hsend.at[last, n], csrecv.at[u], rowdev(-2 if up else 2),
        )

    def detour_on(u, up):
        n = 2 * u + (0 if up else 1)
        return remote(
            sbuf.at[u], ext.at[last, pl.ds(plan[n][3], half)],
            ssend.at[u], hrecv.at[last, n], rowdev(3 if up else -3),
        )

    def share(j, up):
        src, dst, n = (4 * BLOCK, 0, 4) if up else (top, top + tr, 5)
        return remote(
            ext.at[j, pl.ds(src, BLOCK)], ext.at[j, pl.ds(dst, BLOCK)],
            csend.at[j], hrecv.at[j, n], pair,
        )

    def when(cond, act):
        if cond is None:
            act()
        else:
            pl.when(cond)(act)

    def halo_wait(j, n):
        dst = ext.at[j, pl.ds(plan[n][3], plan[n][2])]
        pltpu.make_async_copy(dst, dst, hrecv.at[j, n]).wait()

    def fan(devs, first):
        return [
            pltpu.make_async_remote_copy(
                src_ref=pbuf, dst_ref=pbuf, send_sem=dsend.at[first + k], recv_sem=drecv,
                device_id=dev, device_id_type=MESH,
            )
            for k, dev in enumerate(devs)
        ]

    def forward(cond, devs, first, start):
        @pl.when(cond)
        def _():
            for cp in fan(devs, first):
                if start:
                    cp.start()
                else:
                    cp.wait_send()

    def forwards(start, at_root):
        at = is_root if at_root else jnp.logical_not(is_root)
        if at_root:
            forward(at, [peer], 4, start)
        forward(both(hub, at), xdevs, 1, start)
        forward(both(same_core, at), [pair], 0, start)

    @pl.when(is_root)
    def _():
        fan([peer], 4)[0].start()

    for u in range(2):
        when(seam_up, lambda: detour(u, True).start())
        when(seam_down, lambda: detour(u, False).start())
    for n in range(len(plan)):
        when(who[0][n], lambda: halo(0, n).start())

    @pl.when(both(hub, jnp.logical_not(is_root)))
    def _():
        fan([pair], 0)[0].wait_recv()

    @pl.when(hub)
    def _():
        for cp in fan(xdevs, 1) + fan([pair], 0):
            cp.start()

    for n in range(len(plan)):
        when(who[1][n], lambda: halo(1, n).start())

    @pl.when(leaf)
    def _():
        fan([pair], 0)[0].wait_recv()
        fan([pair], 0)[0].start()

    for u in range(2):
        def act(up):
            src = sbuf.at[u]
            pltpu.make_async_copy(src, src, csrecv.at[u]).wait()
            detour_on(u, up).start()

        when(via_up, lambda: act(True))
        when(via_down, lambda: act(False))

    for cp in loads:
        cp.wait()

    def split(v):
        hi = v.astype(jnp.bfloat16)
        return hi, (v - hi.astype(jnp.float32)).astype(jnp.bfloat16)

    def put_h(i, t, v):
        hi, lo = split(v)
        hs[pl.ds(i * BLOCK, BLOCK), pl.ds(t * BLOCK, BLOCK)] = hi
        hs[pl.ds(tr + i * BLOCK, BLOCK), pl.ds(t * BLOCK, BLOCK)] = lo

    def put_e(j, start, size):
        hi, lo = split(ext[j, pl.ds(start, size)])
        ehi[j, pl.ds(start, size)] = hi
        elo[j, pl.ds(start, size)] = lo

    for i in range(ROWB):
        row = ROWB * r + i
        slots = [
            jnp.bitwise_and(cols[k, row] - row + nb // 2, nb - 1) - nb // 2 + REACH
            for k in range(nnz)
        ]
        for o in range(BAND):
            which = jnp.int32(nnz)
            for k in range(nnz):
                which = jnp.where(slots[k] == o, k, which)
            put_h(i, i + o, cbuf[i, which])
        for t in range(EXT):
            if t < i or t > i + BAND - 1:
                zero = jnp.zeros((BLOCK, BLOCK), jnp.bfloat16)
                hs[pl.ds(i * BLOCK, BLOCK), pl.ds(t * BLOCK, BLOCK)] = zero
                hs[pl.ds(tr + i * BLOCK, BLOCK), pl.ds(t * BLOCK, BLOCK)] = zero

    for j in range(COLB):
        put_e(j, REACH * BLOCK, tr)

    @pl.when(jnp.logical_not(same_core))
    def _():
        fan([pair], 0)[0].wait_recv()

    def dot_t(a, b):
        return lax.dot_general(
            a, b, (((1,), (1,)), ((), ())), preferred_element_type=jnp.float32
        )

    own_at = pl.ds(REACH * BLOCK, tr)
    for j in range(COLB):
        dhi, dlo = split(onsite[COLB * c + j] * unpack(pbuf[j]))
        yhi = ehi[j, own_at]
        dterm[j] = dot_t(yhi, dhi) + dot_t(yhi, dlo) + dot_t(elo[j, own_at], dhi)

    side = lax.rem(c, 2)

    def deliver(src, dev, j, ssem):
        return remote(src, tbuf.at[side, j], ssem, trecv.at[side, j], dev)

    def mine_of(k, j):
        return lbuf.at[j, pl.ds(part(k, c) * half, half)]

    def straight(k, j):
        return deliver(mine_of(k, j), goal(k, r, c), j, tsend.at[k, j])

    def inside(k, j):
        return pltpu.make_async_copy(mine_of(k, j), tbuf.at[side, j], trecv.at[side, j])

    def to_relay(k, j):
        slot = lax.rem(r // 2, 2) if k == 0 else lax.rem(r // 4, 2)
        return remote(
            mine_of(k, j), rbuf.at[k, slot, j], tsend.at[k, j], rrecv.at[k, slot, j],
            relay(k, r, c),
        )

    def onward(k, s, j):
        return deliver(rbuf.at[k, s, j], goal(k, *sources[k][s]), j, fsend.at[k, s, j])

    def to_far(s):
        return remote(
            rbuf.at[1, s, 0], fbuf.at[s], fsend.at[1, s, 0], frecv.at[s], around(r, c)
        )

    def from_far(s):
        return deliver(fbuf.at[s], goal(1, *far_sources[s]), 0, osend.at[s])

    def passing(k, s, j, act):
        if (k, j) == (1, 0):
            when(mid, lambda: act(to_far(s)))
            when(jnp.logical_not(mid), lambda: act(onward(k, s, j)))
        else:
            act(onward(k, s, j))

    at_home = [is_me(goal(k, r, c)) for k in range(2)]

    def product(j, start, size):
        at = pl.ds(pl.multiple_of(start, BLOCK), size)
        high = ehi[j, at]
        p = jnp.dot(hs[:, at], high, preferred_element_type=jnp.float32)
        q = jnp.dot(hs[pl.ds(0, tr), at], elo[j, at], preferred_element_type=jnp.float32)
        return p[:tr] + p[tr:] + q

    def by_core(a, b):
        return jnp.where(even, a, b).astype(i32)

    for j in range(COLB):
        @pl.when(even)
        def _():
            halo_wait(j, 1)
            halo_wait(j, 3)
            put_e(j, top, tr)

        @pl.when(odd)
        def _():
            halo_wait(j, 0)
            halo_wait(j, 2)
            put_e(j, BLOCK, tr)

        dterm[j] = dterm[j] + product(j, by_core(REACH * BLOCK, BLOCK), 2 * tr)

    for j in range(COLB):
        @pl.when(even)
        def _():
            halo_wait(j, 0)
            share(j, True).start()
            halo_wait(j, 2)
            halo_wait(j, 4)
            put_e(j, 0, REACH * BLOCK)
            halo_wait(j, 5)
            put_e(j, top + tr, BLOCK)

        @pl.when(odd)
        def _():
            halo_wait(j, 3)
            share(j, False).start()
            halo_wait(j, 1)
            halo_wait(j, 5)
            put_e(j, top, REACH * BLOCK)
            halo_wait(j, 4)
            put_e(j, 0, BLOCK)

        far = product(j, by_core(0, top), REACH * BLOCK)
        lbuf[j] = dterm[j] + far + product(j, by_core(top + tr, 0), BLOCK)

        for k in range(2):
            @pl.when(at_home[k])
            def _():
                inside(k, j).start()

            @pl.when(both(direct[k], jnp.logical_not(at_home[k])))
            def _():
                straight(k, j).start()

            @pl.when(jnp.logical_not(direct[k]))
            def _():
                to_relay(k, j).start()

    def forward_on(k, j):
        for s in range(2):
            @pl.when(serves[k][s])
            def _():
                src = rbuf.at[k, s, j]
                pltpu.make_async_copy(src, src, rrecv.at[k, s, j]).wait()
                passing(k, s, j, lambda cp: cp.start())

    forward_on(0, 0)

    @pl.when(gives)
    def _():
        for j in range(COLB):
            to_relay(0, j).wait_send()
        pl.semaphore_signal(token, inc=1, device_id=taker, device_id_type=MESH)

    forward_on(1, 0)
    forward_on(0, 1)

    @pl.when(takes)
    def _():
        pl.semaphore_wait(token, 1)

    forward_on(1, 1)

    for s in range(2):
        @pl.when(far_serves[s])
        def _():
            src = fbuf.at[s]
            pltpu.make_async_copy(src, src, frecv.at[s]).wait()
            from_far(s).start()

    for j in range(COLB):
        for g in range(2):
            dst = tbuf.at[g, j]
            pltpu.make_async_copy(dst, dst, trecv.at[g, j]).wait()
            rows = pl.ds((2 * g + j) * BLOCK, BLOCK)
            here = pl.ds((REACH + 2 * g + j) * BLOCK, BLOCK)
            turned = tbuf[g, j].T
            for b in range(COLB):
                lanes = pl.ds(b * BLOCK, BLOCK)
                mine = lbuf[b, rows] - turned[:, b * BLOCK:(b + 1) * BLOCK]
                out[rows, lanes] = ext[b, here] + STEP * mine

    for j in range(COLB):
        for n in range(len(plan)):
            when(who[j][n], lambda: halo(j, n).wait_send())
        when(even, lambda: share(j, True).wait_send())
        when(jnp.logical_not(even), lambda: share(j, False).wait_send())
    for u in range(2):
        when(seam_up, lambda: detour(u, True).wait_send())
        when(seam_down, lambda: detour(u, False).wait_send())
        when(via_up, lambda: detour_on(u, True).wait_send())
        when(via_down, lambda: detour_on(u, False).wait_send())
    for s in range(2):
        when(far_serves[s], lambda: from_far(s).wait_send())
    forwards(False, True)
    forwards(False, False)
    for j in range(COLB):
        for k in range(2):
            @pl.when(both(direct[k], jnp.logical_not(at_home[k])))
            def _():
                straight(k, j).wait_send()

            left = jnp.logical_not(direct[k])
            if k == 0:
                left = both(left, jnp.logical_not(gives))

            @pl.when(left)
            def _():
                to_relay(k, j).wait_send()

            for s in range(2):
                @pl.when(serves[k][s])
                def _():
                    passing(k, s, j, lambda cp: cp.wait_send())


def solution(mesh):
    nrow = mesh.shape["row"]

    def on_device(covariance, couplings, block_columns, onsite):
        rows, width = covariance.shape
        nb, nnz = block_columns.shape
        f32, bf16 = jnp.float32, jnp.bfloat16
        dma = pltpu.SemaphoreType.DMA
        return pl.pallas_call(
            functools.partial(kernel, nrow, nb, nnz),
            out_shape=jax.ShapeDtypeStruct((rows, width), f32),
            in_specs=[pl.BlockSpec(memory_space=pl.ANY)] * 4,
            out_specs=pl.BlockSpec(memory_space=pltpu.VMEM),
            scratch_shapes=[
                pltpu.SMEM((nnz, nb), jnp.int32),
                pltpu.SMEM((nb,), f32),
                pltpu.VMEM((COLB, EXT * BLOCK, BLOCK), f32),
                pltpu.VMEM((ROWB, nnz + 1, BLOCK, BLOCK), f32),
                pltpu.VMEM((COLB, BLOCK, BLOCK), f32),
                pltpu.VMEM((COLB, BLOCK // 2, BLOCK), f32),
                pltpu.VMEM((COLB, rows, BLOCK), f32),
                pltpu.VMEM((COLB, EXT * BLOCK, BLOCK), bf16),
                pltpu.VMEM((COLB, EXT * BLOCK, BLOCK), bf16),
                pltpu.VMEM((2 * rows, EXT * BLOCK), bf16),
                pltpu.VMEM((COLB, rows, BLOCK), f32),
                pltpu.VMEM((2, 2, COLB, 2 * BLOCK, BLOCK), f32),
                pltpu.VMEM((COLB, 2 * BLOCK, BLOCK), f32),
                pltpu.VMEM((2, COLB, 2 * BLOCK, BLOCK), f32),
                dma((7,)), dma((COLB, 6)), dma((COLB, 6)), dma((COLB,)), dma((2,)), dma((2,)),
                dma((5,)), dma(()),
                dma((2, COLB)), dma((2, 2, COLB)), dma((2, 2, COLB)), dma((2, COLB)),
                pltpu.SemaphoreType.REGULAR,
                pltpu.VMEM((2, 2 * BLOCK, BLOCK), f32), dma((2,)), dma((2,)),
            ],
            compiler_params=pltpu.CompilerParams(
                collective_id=0, has_side_effects=True, vmem_limit_bytes=63 * 2**20
            ),
        )(covariance, couplings, block_columns.T, onsite)

    return jax.shard_map(
        on_device,
        mesh=mesh,
        in_specs=(P("row", "col"), P("row", None, None, None), P(), P()),
        out_specs=P("row", "col"),
        check_vma=False,
    )
```
